32 devices in a mesh: space: 4 (over y, x), vel: 8 (over z, core).
Axes of the slice: x: 2, y: 2, z: 4, core: 2. Of those that a mesh axis runs over, the one named last changes fastest.
Arguments:
- distribution: float32 [256, 64, 4096], P('space', None, 'vel'), may hold values from -6 to 6
- inverse_jacobian: float32 [256, 3, 3], P('space'), may hold values from -1 to 1
- density: float32 [256, 64], P('space'), may hold values from 1 to 10
- collision_blocks: float32 [32, 6, 128, 128], replicated, may hold values from -0.21875 to 0.21875
- block_columns: int32 [32, 6], replicated, may hold values from 0 to 31, as said below
- send_lists: int32 [4, 4, 48], P('space'), may hold values from 0 to 383, as said below
- exterior_faces: int32 [256, 6], P('space'), may hold values from 0 to 576, as said below
Outputs:
- advanced: float32 [256, 64, 4096], P('space', None, 'vel')
The draws below stay inside these ranges and needn't reach their ends.
Inputs may be any that keep to these rules, and one draw needn't show every extreme that they name: `block_columns`: each row b lists 6 different block columns, the first being b itself. send_lists[q, p] holds different faces (6 e + s, e local to q) in its first slots and 0 in the slots after them; send_lists[p, p] is all 0. Every used slot is read by exactly one face of partition p, and slots after the used ones are read by none. `exterior_faces`: an entry below 384 names a face 6 e + s of the partition's own elements; 384 + q * 48 + j names slot j of the list partition q sends to this partition; 576 marks a wall, whose exterior trace is zero. Exactly 32 faces of each partition are walls.
All inputs are finite; a program needn't handle non-finite values.
Results may differ from the reference program's by a relative error of at most 0.0003.
Values sent between devices are 32-bit elements; how exact they have to be, the bound alone decides.
No kernel may reach another device: no remote copies, remote signals or barrier semaphores. Data moves between devices by JAX's collectives and lax.ppermute only.
A program may use at most 256 MiB of HBM per device.

```python
import math
import jax
import jax.numpy as jnp
import numpy as np
from jax import lax

E_DEV = 64
NODES = 64
VG = 16
BS = 128
KB = 6
NV = 4096
NB = 32
CAP = 48
WALLS = 32
E_TOT = 256
N_SPACE = 4


def mesh_tables(key):
    face_count = 6 * E_DEV
    part_count = N_SPACE
    wall_value = face_count + part_count * CAP
    counts = jax.random.randint(jax.random.fold_in(key, 11), (part_count, part_count), CAP // 2, CAP + 1)
    pair_pick = jax.random.randint(jax.random.fold_in(key, 12), (), 0, part_count * (part_count - 1))
    source = pair_pick // (part_count - 1)
    offset = pair_pick % (part_count - 1)
    target = offset + (offset >= source).astype(jnp.int32)
    row_ids = jnp.arange(part_count)[:, None]
    col_ids = jnp.arange(part_count)[None, :]
    forced = (row_ids == source) & (col_ids == target)
    counts = jnp.where(forced, CAP, counts)
    counts = jnp.where(row_ids == col_ids, 0, counts)
    list_keys = jax.random.split(jax.random.fold_in(key, 13), part_count * part_count)

    def one_list(list_key):
        return jax.random.permutation(list_key, face_count).astype(jnp.int32)[:CAP]
    shuffled = jax.vmap(one_list)(list_keys).reshape(part_count, part_count, CAP)
    swapped = jnp.where(shuffled == face_count - 1, shuffled[:, :, :1], shuffled)
    swapped = jnp.concatenate([jnp.full((part_count, part_count, 1), face_count - 1, jnp.int32), swapped[:, :, 1:]], 2)
    shuffled = jnp.where(forced[:, :, None], swapped, shuffled)
    slot_ids = jnp.arange(CAP)[None, None, :]
    lists = jnp.where(slot_ids < counts[:, :, None], shuffled, 0).astype(jnp.int32)
    exterior_parts = []
    for dest in range(part_count):
        incoming = counts[:, dest]
        slot_ends = jnp.cumsum(incoming)
        slot_starts = slot_ends - incoming
        remote_total = slot_ends[part_count - 1]
        role_ids = jnp.arange(face_count, dtype=jnp.int32)
        remote = role_ids - WALLS
        source_of = jnp.sum((remote[:, None] >= slot_ends[None, :]).astype(jnp.int32), axis=1)
        source_of = jnp.minimum(source_of, part_count - 1)
        slot_of = remote - jnp.take(slot_starts, source_of)
        local_values = jax.random.randint(jax.random.fold_in(key, 40 + dest), (face_count,), 0, face_count)
        local_values = jnp.where(role_ids == WALLS + remote_total, 0, local_values)
        values = jnp.where(role_ids < WALLS, wall_value, jnp.where(remote < remote_total, face_count + source_of * CAP + slot_of, local_values))
        face_order = jax.random.permutation(jax.random.fold_in(key, 30 + dest), face_count).astype(jnp.int32)
        inverse = jnp.argsort(face_order)
        exterior_parts.append(values[inverse].reshape(E_DEV, 6))
    exterior = jnp.concatenate(exterior_parts, 0).astype(jnp.int32)
    return (lists, exterior)


def draw_send_lists(key, part):
    return mesh_tables(key)[0]


def draw_exterior_faces(key, part):
    return mesh_tables(key)[1]


def draw_block_columns(key, part):
    row_keys = jax.random.split(jax.random.fold_in(key, 5), NB)

    def one_row(row_key):
        return jax.random.permutation(row_key, NB - 1).astype(jnp.int32)[:KB - 1]
    others = jax.vmap(one_row)(row_keys)
    row_ids = jnp.arange(NB, dtype=jnp.int32)[:, None]
    return jnp.concatenate([row_ids, (row_ids + 1 + others) % NB], 1).astype(jnp.int32)


def block_scale(own_key, dims, pieces, least, top_value):
    loudness, own = 1.0, jax.random.fold_in(own_key, 6)
    for position, shards_of in pieces:
        heights = jnp.exp(jax.random.uniform(jax.random.fold_in(own, position), (shards_of,), jnp.float32, least / len(pieces), top_value / len(pieces)))
        loudness = loudness * jnp.repeat(heights, dims[position] // shards_of).reshape([-1 if axis == position else 1 for axis in range(len(dims))])
    return loudness


def noise(stream_key, dims, scale, most, cuts=(), held_as=jnp.bfloat16):
    values = jax.random.normal(stream_key, dims, jnp.float32) * scale
    if len(cuts) > 0:
        values = block_scale(stream_key, dims, cuts, -0.22, 0.18) * values
    return jnp.clip(values, min=-most, max=most).astype(held_as)


def setup_inputs(seed: int = 0) -> dict:
    keys = jax.random.split(jax.random.key(seed), 8)
    return {
        "distribution": noise(keys[0], (E_TOT, NODES, NV), 1.0, 6.0, ((0, 4), (2, 8)), jnp.float32),
        "inverse_jacobian": jnp.clip(jax.random.uniform(keys[1], (E_TOT, 3, 3), jnp.float32, -1.0, 1.0) * block_scale(keys[1], (E_TOT, 3, 3), ((0, 4),), -0.4, 0.0), -1.0, 1.0),
        "density": jnp.clip(jnp.exp(math.log(10.0) - 2.3025851 * jax.random.uniform(keys[2], (E_TOT, NODES), jnp.float32) ** block_scale(keys[2], (E_TOT, NODES), ((0, 4),), -0.2, 0.2)), 1.0, 10.0),
        "collision_blocks": noise(keys[3], (NB, KB, BS, BS), (KB * BS) ** -0.5, 0.21875, (), jnp.float32),
        "block_columns": draw_block_columns(jax.random.fold_in(keys[7], 71), 0),
        "send_lists": draw_send_lists(jax.random.fold_in(keys[7], 71), 0),
        "exterior_faces": draw_exterior_faces(jax.random.fold_in(keys[7], 71), 0),
    }


TIME_STEP = 0.03
LIFT_SCALE = 6.0

def lagrange_derivative():
    points = np.array([-1.0, -1.0 / np.sqrt(5.0), 1.0 / np.sqrt(5.0), 1.0])
    barycentric = np.ones(4)
    for column in range(4):
        for second in range(4):
            if second != column:
                barycentric[column] = barycentric[column] / (points[column] - points[second])
    matrix = np.zeros((4, 4))
    for row_node in range(4):
        for col_node in range(4):
            if row_node != col_node:
                matrix[row_node, col_node] = barycentric[col_node] / barycentric[row_node] / (points[row_node] - points[col_node])
        matrix[row_node, row_node] = -np.sum(matrix[row_node])
    return matrix

def derivative_stack():
    single = lagrange_derivative()
    identity = np.eye(4)
    stacked = np.concatenate([np.kron(np.kron(single, identity), identity), np.kron(np.kron(identity, single), identity), np.kron(np.kron(identity, identity), single)], 0)
    return jnp.asarray(stacked, dtype=jnp.float32)

def grid_velocities(first_id, amount):
    velocity_id = first_id + jnp.arange(amount, dtype=jnp.int32)
    components = [velocity_id // (VG * VG), velocity_id // VG % VG, velocity_id % VG]
    return [3.0 * ((2.0 * component.astype(jnp.float32) + 1.0) / VG - 1.0) for component in components]

def face_speeds(inverse_jacobian, velocity_x, velocity_y, velocity_z):
    return inverse_jacobian[:, :, 0, None] * velocity_x[None, None, :] + inverse_jacobian[:, :, 1, None] * velocity_y[None, None, :] + inverse_jacobian[:, :, 2, None] * velocity_z[None, None, :]

def face_values(node_field):
    node_cube = node_field.reshape(node_field.shape[0], 4, 4, 4, node_field.shape[2])
    face_list = [node_cube[:, 0], node_cube[:, 3], node_cube[:, :, 0], node_cube[:, :, 3], node_cube[:, :, :, 0], node_cube[:, :, :, 3]]
    return jnp.stack(face_list, 1).reshape(node_field.shape[0], 6, 16, node_field.shape[2])

def lift_faces(face_flux):
    elements = face_flux.shape[0]
    columns = face_flux.shape[3]
    blocks = face_flux.reshape(elements, 6, 4, 4, columns)
    summed = jnp.zeros((elements, 4, 4, 4, columns), jnp.float32)
    for face_id in range(6):
        direction = face_id // 2
        placed = jnp.expand_dims(blocks[:, face_id], 1 + direction)
        padding = [(0, 0), (0, 0), (0, 0), (0, 0), (0, 0)]
        padding[1 + direction] = (0, 3) if face_id % 2 == 0 else (3, 0)
        summed = summed + jnp.pad(placed, padding)
    return summed.reshape(elements, 64, columns)

def advection(node_field, speeds, interior, outside):
    stacked = derivative_stack()
    derived = jnp.einsum('mn,env->emv', stacked, node_field, precision=lax.Precision.HIGHEST)
    derived = derived.reshape(node_field.shape[0], 3, node_field.shape[1], node_field.shape[2])
    volume = -(speeds[:, 0, None, :] * derived[:, 0] + speeds[:, 1, None, :] * derived[:, 1] + speeds[:, 2, None, :] * derived[:, 2])
    face_signs = jnp.asarray(np.array([-1.0, 1.0, -1.0, 1.0, -1.0, 1.0]), dtype=jnp.float32)
    normal = jnp.repeat(speeds, 2, axis=1) * face_signs[None, :, None]
    weight = LIFT_SCALE * jnp.minimum(normal, 0.0)
    face_flux = weight[:, :, None, :] * (interior - outside)
    return volume + lift_faces(face_flux)

def reference(distribution, inverse_jacobian, density, collision_blocks, block_columns, send_lists, exterior_faces):

    def advect_block(block_pair):
        block, first_id = block_pair
        velocity = grid_velocities(first_id, BS)
        speeds = face_speeds(inverse_jacobian, velocity[0], velocity[1], velocity[2])
        interior = face_values(block)
        part_faces = interior.reshape(N_SPACE, E_DEV * 6, 16, BS)
        outside_parts = []
        for target in range(N_SPACE):
            received = [jnp.take(part_faces[source], send_lists[source, target], axis=0) for source in range(N_SPACE)]
            face_table = jnp.concatenate([part_faces[target]] + received + [jnp.zeros((1, 16, BS), jnp.float32)], 0)
            lookup = exterior_faces[target * E_DEV:(target + 1) * E_DEV].reshape(-1)
            outside_parts.append(jnp.take(face_table, lookup, axis=0))
        outside = jnp.concatenate(outside_parts, 0).reshape(interior.shape)
        return advection(block, speeds, interior, outside)

    def advect_all(node_field):
        blocks = jnp.moveaxis(node_field.reshape(E_TOT, NODES, NB, BS), 2, 0)
        starts = jnp.arange(NB, dtype=jnp.int32) * BS
        result = lax.map(advect_block, (blocks, starts))
        return jnp.moveaxis(result, 0, 2).reshape(E_TOT, NODES, NV)

    def collide_all(node_field):
        row_blocks = node_field.reshape(-1, NB, BS)

        def per_block(block_id):
            gathered = jnp.take(row_blocks, block_columns[block_id], axis=1)
            return jnp.einsum('rkj,kij->ri', gathered, collision_blocks[block_id], precision=lax.Precision.HIGHEST)
        result = lax.map(per_block, jnp.arange(NB, dtype=jnp.int32))
        applied = jnp.moveaxis(result, 0, 1).reshape(node_field.shape)
        return applied - node_field

    def rate(node_field):
        return advect_all(node_field) + density[:, :, None] * collide_all(node_field)
    first_section = distribution + TIME_STEP * rate(distribution)
    return 0.5 * distribution + 0.5 * (first_section + TIME_STEP * rate(first_section))
```

```python
import functools

import jax
import jax.numpy as jnp
import numpy as np
from jax import lax
from jax.experimental import pallas as pl
from jax.experimental.pallas import tpu as pltpu
from jax.sharding import PartitionSpec as P

VG = 16
SIDE = 4
FACES = 6
FACE_NODES = 16
LANES = 128

TIME_STEP = 0.03
LIFT_SCALE = 6.0


MIB = 1024 * 1024


def lagrange_derivative():
    points = np.array([-1.0, -1.0 / np.sqrt(5.0), 1.0 / np.sqrt(5.0), 1.0])
    barycentric = np.ones(4)
    for column in range(4):
        for second in range(4):
            if second != column:
                barycentric[column] = barycentric[column] / (points[column] - points[second])
    matrix = np.zeros((4, 4))
    for row_node in range(4):
        for col_node in range(4):
            if row_node != col_node:
                matrix[row_node, col_node] = (
                    barycentric[col_node]
                    / barycentric[row_node]
                    / (points[row_node] - points[col_node])
                )
        matrix[row_node, row_node] = -np.sum(matrix[row_node])
    return matrix


def derivative_parts():
    single = lagrange_derivative()
    identity = np.eye(4)
    stacked = np.concatenate(
        [
            np.kron(np.kron(single, identity), identity),
            np.kron(np.kron(identity, single), identity),
            np.kron(np.kron(identity, identity), single),
        ],
        0,
    ).astype(np.float32)
    high = stacked.astype(jnp.bfloat16)
    low = (stacked - high.astype(np.float32)).astype(jnp.bfloat16)
    return np.concatenate([high, high, low], 1)


def lift_parts():
    nodes = SIDE**3
    place = np.zeros((nodes, 3, 2, FACE_NODES), np.float32)
    for node in range(nodes):
        index = (node // 16, node // 4 % 4, node % 4)
        for direction in range(3):
            others = [index[d] for d in range(3) if d != direction]
            if index[direction] == 0:
                place[node, direction, 0, others[0] * 4 + others[1]] = 1.0
            if index[direction] == SIDE - 1:
                place[node, direction, 1, others[0] * 4 + others[1]] = 1.0
    place = place.reshape(nodes, 6 * FACE_NODES).astype(jnp.bfloat16)
    return np.concatenate([place, place], 1)


def shell():
    nodes = np.ndindex(SIDE, SIDE, SIDE)
    return [index for index in nodes if 0 in index]


SHELL = len(shell())
SHELL_MAIN = SHELL // 32 * 32
SHELL_ROWS = -(-SHELL // 8) * 8


def turned(index, flip):
    return tuple(SIDE - 1 - i if f else i for i, f in zip(index, flip))


def pack_parts():
    rows = {index: row for row, index in enumerate(shell())}
    pack = np.zeros((SHELL_ROWS, 3, 2, 2, FACE_NODES), np.float32)
    for direction in range(3):
        for first, second, a, b in np.ndindex(2, 2, SIDE, SIDE):
            where = list(turned((a, b), (first, second)))
            where.insert(direction, 0)
            pack[rows[tuple(where)], direction, first, second, a * SIDE + b] = 1.0
    pack = pack.reshape(SHELL_ROWS, -1).astype(jnp.bfloat16)
    return np.concatenate([pack, pack], 1)


def spread_parts():
    spread = np.zeros((SIDE, SIDE, SIDE, 2, 2, 2, SHELL_ROWS), np.float32)
    for flip in np.ndindex(2, 2, 2):
        for row, index in enumerate(shell()):
            spread[turned(index, flip) + flip + (row,)] = 1.0
    spread = spread.reshape(SIDE**3, -1).astype(jnp.bfloat16)
    return np.concatenate([spread, spread], 1)


def grid_velocities(first_id, amount):
    velocity_id = first_id + jnp.arange(amount, dtype=jnp.int32)
    components = [velocity_id // (VG * VG), velocity_id // VG % VG, velocity_id % VG]
    return jnp.stack(
        [3.0 * ((2.0 * component.astype(jnp.float32) + 1.0) / VG - 1.0) for component in components]
    )


def halves(value):
    high = value.astype(jnp.bfloat16)
    return high, (value - high.astype(jnp.float32)).astype(jnp.bfloat16)


def speeds_of(jacobian_ref, element, velocity):
    result = []
    for direction in range(3):
        base = element * 9 + direction * 3
        result.append(
            jacobian_ref[base] * velocity[0:1]
            + jacobian_ref[base + 1] * velocity[1:2]
            + jacobian_ref[base + 2] * velocity[2:3]
        )
    return result


def lifted(fluxes, speeds, lift):
    pieces = []
    for flux, speed in zip(fluxes, speeds):
        inward = speed > 0.0
        pieces.append(jnp.where(inward, flux, 0.0))
        pieces.append(jnp.where(inward, 0.0, flux))
    high, low = halves(jnp.concatenate(pieces, 0))
    return jnp.dot(lift, jnp.concatenate([high, low], 0), preferred_element_type=jnp.float32)


def signs(speeds):
    return [(jnp.where(s > 0.0, 1.0, 0.0), jnp.where(s > 0.0, 0.0, 1.0)) for s in speeds]


def packed(fluxes, speeds, pack):
    masks = signs(speeds)
    pieces = []
    for direction, flux in enumerate(fluxes):
        first, second = [masks[d] for d in range(3) if d != direction]
        pieces += [flux * (a * b) for a in first for b in second]
    high, low = halves(jnp.concatenate(pieces, 0))
    return jnp.dot(pack, jnp.concatenate([high, low], 0), preferred_element_type=jnp.float32)


def spread_out(rows, speeds, spread):
    masks = signs(speeds)
    pieces = [rows * (a * b * c) for a in masks[0] for b in masks[1] for c in masks[2]]
    high, low = halves(jnp.concatenate(pieces, 0))
    return jnp.dot(spread, jnp.concatenate([high, low], 0), preferred_element_type=jnp.float32)


def shell_rows(flux_ref, tail_ref, owned, element):
    for row in range(SHELL - SHELL_MAIN):
        at = owned * SHELL_MAIN + row * owned + element
        tail_ref[row : row + 1, :] = flux_ref[0, pl.ds(at, 1), :]
    for row in range(SHELL - SHELL_MAIN, tail_ref.shape[0]):
        tail_ref[row : row + 1, :] = jnp.zeros((1, tail_ref.shape[1]), jnp.float32)
    start = pl.multiple_of(element * SHELL_MAIN, SHELL_MAIN)
    return lambda lanes: jnp.concatenate(
        [flux_ref[0, pl.ds(start, SHELL_MAIN), lanes], tail_ref[:, lanes]], 0
    )


def own_flow(value, speeds, derivative):
    high, low = halves(value)
    slopes = jnp.dot(
        derivative, jnp.concatenate([high, low, high], 0), preferred_element_type=jnp.float32
    )
    node = lax.broadcasted_iota(jnp.int32, value.shape, 0)
    count = value.shape[0]
    total = None
    for direction in range(3):
        speed = speeds[direction]
        place = (node >> (4 - 2 * direction)) & 3
        side = jnp.where(speed > 0.0, 0, SIDE - 1)
        edge = jnp.where(place == side, LIFT_SCALE * jnp.abs(speed), 0.0)
        term = speed * slopes[direction * count : (direction + 1) * count] + edge * value
        total = term if total is None else total + term
    return -total


def lane_chunks(width):
    step = 2 * LANES if width % (2 * LANES) == 0 else LANES
    return [pl.ds(start, step) for start in range(0, width, step)]


def whole(space=pltpu.VMEM):
    return pl.BlockSpec(memory_space=space)


def params(mebibytes):
    return pltpu.CompilerParams(vmem_limit_bytes=mebibytes * MIB)


def cost(flops, moved):
    return pl.CostEstimate(flops=int(flops), bytes_accessed=int(moved), transcendentals=0)


def faces_kernel(cap, others, send_ref, *refs):
    value_ref = refs[0]
    change_ref = refs[1] if len(refs) > others + 2 else None
    table_ref, out_refs = refs[-1 - others], refs[len(refs) - others :]
    elements = value_ref.shape[0]
    surface = surface_nodes()

    def rows(element, start, stop):
        value = value_ref[element, start:stop, :]
        if change_ref is None:
            return value
        at = surface.index(start)
        return value + TIME_STEP * change_ref[element, at : at + stop - start, :]

    def build(element, carry):
        face = element * FACES
        table_ref[face] = rows(element, 0, 16)
        table_ref[face + 1] = rows(element, 48, 64)
        for i in range(SIDE):
            to = slice(4 * i, 4 * i + 4)
            table_ref[face + 2, to, :] = rows(element, 16 * i, 16 * i + 4)
            table_ref[face + 3, to, :] = rows(element, 16 * i + 12, 16 * i + 16)
        for m in range(FACE_NODES):
            to = slice(m, m + 1)
            table_ref[face + 4, to, :] = rows(element, 4 * m, 4 * m + 1)
            table_ref[face + 5, to, :] = rows(element, 4 * m + 3, 4 * m + 4)
        return carry

    lax.fori_loop(0, elements, build, 0)
    for number, out_ref in enumerate(out_refs):

        def pick(slot, carry, number=number, out_ref=out_ref):
            out_ref[slot] = table_ref[send_ref[number * cap + slot]]
            return carry

        lax.fori_loop(0, cap, pick, 0)


def faces(values, send_ids, others, cap):
    elements, _, width = values[0].shape
    out_shape = [jax.ShapeDtypeStruct((FACES * elements, FACE_NODES, width), jnp.float32)]
    out_shape += [jax.ShapeDtypeStruct((cap, FACE_NODES, width), jnp.float32)] * others
    moved = sum(value.size for value in values)
    moved += width * FACE_NODES * (FACES * elements + others * cap)
    return pl.pallas_call(
        functools.partial(faces_kernel, cap, others),
        out_shape=out_shape,
        in_specs=[whole(pltpu.SMEM)] + [whole()] * len(values),
        out_specs=[whole()] * (1 + others),
        compiler_params=params(44),
        cost_estimate=cost(0, 8 * moved),
        name="faces",
    )(send_ids, *values)


def inflow_kernel(scale, lookup_ref, jacobian_ref, velocity_ref, lift_ref, table_ref, in_ref, out_ref):
    local = table_ref.shape[0]
    remote = in_ref.shape[0]
    elements = local // FACES
    velocity = velocity_ref[...]

    def one(element, carry):
        speeds = speeds_of(jacobian_ref, element, velocity)
        fluxes = []
        for direction in range(3):
            traces = []
            for side in range(2):
                index = lookup_ref[element * FACES + 2 * direction + side]
                near = table_ref[jnp.minimum(index, local - 1)]
                far = in_ref[jnp.clip(index - local, 0, remote - 1)]
                far = jnp.where(index < local + remote, far, 0.0)
                traces.append(jnp.where(index < local, near, far))
            speed = speeds[direction]
            fluxes.append(
                (LIFT_SCALE * jnp.abs(speed)) * jnp.where(speed > 0.0, traces[0], traces[1])
            )
        if scale is None:
            owned = elements // out_ref.shape[0]
            owner, own = lax.div(element, owned), lax.rem(element, owned)
            rows = packed(fluxes, speeds, lift_ref[...])
            start = pl.multiple_of(own * SHELL_MAIN, SHELL_MAIN)
            out_ref[owner, pl.ds(start, SHELL_MAIN), :] = rows[:SHELL_MAIN]
            for row in range(SHELL_MAIN, SHELL):
                at = owned * SHELL_MAIN + (row - SHELL_MAIN) * owned + own
                out_ref[owner, pl.ds(at, 1), :] = rows[row : row + 1]
        else:
            out_ref[element] = scale * lifted(fluxes, speeds, lift_ref[...])
        return carry

    lax.fori_loop(0, elements, one, 0)


def inflow(table, incoming, lookup, jacobian, velocity, lift, scale, owners):
    width = table.shape[2]
    elements = table.shape[0] // FACES
    shape = (elements, SIDE**3, width)
    if scale is None:
        shape = (owners, elements // owners * SHELL, width)
    moved = table.size + incoming.size + np.prod(shape)
    return pl.pallas_call(
        functools.partial(inflow_kernel, scale),
        out_shape=jax.ShapeDtypeStruct(shape, jnp.float32),
        in_specs=[whole(pltpu.SMEM)] * 2 + [whole()] * 4,
        out_specs=whole(),
        compiler_params=params(36),
        cost_estimate=cost(0, 8 * moved),
        name="inflow",
    )(lookup, jacobian, velocity, lift, table, incoming)


def guess_kernel(
    owned, jacobian_ref, velocity_ref, derivative_ref, spread_ref, value_ref, flux_ref, out_ref, tail_ref
):
    element = pl.program_id(0)
    shell_of = shell_rows(flux_ref, tail_ref, owned, lax.rem(element, owned))
    for lanes in lane_chunks(value_ref.shape[2]):
        value = value_ref[0, :, lanes]
        speeds = speeds_of(jacobian_ref, element, velocity_ref[:, lanes])
        entering = spread_out(shell_of(lanes), speeds, spread_ref[...])
        flow = own_flow(value, speeds, derivative_ref[...]) + entering
        out_ref[0, :, lanes] = value + TIME_STEP * flow


def guess(value, flux, jacobian, velocity, derivative, spread):
    elements, nodes, width = value.shape
    owners, rows, _ = flux.shape
    owned = elements // owners
    return pl.pallas_call(
        functools.partial(guess_kernel, owned),
        grid=(elements,),
        out_shape=jax.ShapeDtypeStruct(value.shape, jnp.float32),
        in_specs=[
            whole(pltpu.SMEM),
            whole(),
            whole(),
            whole(),
            pl.BlockSpec((1, nodes, width), lambda e: (e, 0, 0)),
            pl.BlockSpec((1, rows, width), lambda e: (e // owned, 0, 0)),
        ],
        out_specs=pl.BlockSpec((1, nodes, width), lambda e: (e, 0, 0)),
        scratch_shapes=[pltpu.VMEM((SHELL_ROWS - SHELL_MAIN, width), jnp.float32)],
        compiler_params=params(16),
        cost_estimate=cost(2 * 256 * 192 * value.size // 64, 4 * (2 * value.size + flux.size)),
        name="guess",
    )(jacobian, velocity, derivative, spread, value, flux)


def stage_kernel(
    jacobian_ref,
    velocity_ref,
    derivative_ref,
    spread_ref,
    value_ref,
    flux_ref,
    change_ref,
    first_ref,
    rest_ref,
    tail_ref,
):
    element = pl.program_id(1)
    shell_of = shell_rows(flux_ref, tail_ref, pl.num_programs(1), element)
    for lanes in lane_chunks(value_ref.shape[3]):
        value = value_ref[0, 0, :, lanes]
        speeds = speeds_of(jacobian_ref, element, velocity_ref[0, :, lanes])
        entering = spread_out(shell_of(lanes), speeds, spread_ref[...])
        flow = own_flow(value, speeds, derivative_ref[...]) + entering
        first = value + TIME_STEP * (flow + change_ref[0, 0, :, lanes])
        first_ref[0, 0, :, lanes] = first
        again = own_flow(first, speeds, derivative_ref[...])
        rest_ref[0, 0, :, lanes] = 0.5 * value + 0.5 * (first + TIME_STEP * again)


def stage(value, flux, change, jacobian, velocities, derivative, spread):
    chunks, elements, nodes, width = value.shape
    rows = flux.shape[1]
    block = pl.BlockSpec((1, 1, nodes, width), lambda c, e: (c, e, 0, 0))
    return pl.pallas_call(
        stage_kernel,
        grid=(chunks, elements),
        out_shape=[jax.ShapeDtypeStruct(value.shape, jnp.float32)] * 2,
        in_specs=[
            whole(pltpu.SMEM),
            pl.BlockSpec((1, 3, width), lambda c, e: (c, 0, 0)),
            whole(),
            whole(),
            block,
            pl.BlockSpec((1, rows, width), lambda c, e: (c, 0, 0)),
            block,
        ],
        out_specs=[block, block],
        scratch_shapes=[pltpu.VMEM((SHELL_ROWS - SHELL_MAIN, width), jnp.float32)],
        compiler_params=params(16),
        cost_estimate=cost(2 * 450 * 192 * value.size // 64, 4 * (4 * value.size + flux.size)),
        name="stage",
    )(jacobian, velocities, derivative, spread, value, flux, change)


def collide_kernel(slots, scale, column_ref, *refs):
    piece_refs = refs[:slots]
    weight_ref, density_ref = refs[slots : slots + 2]
    out_ref = refs[slots + 2 + (scale is not None)]
    pieces = [ref[0] for ref in piece_refs]
    high, low = halves(jnp.concatenate(pieces, 1))
    weight_high, weight_low = halves(
        jnp.concatenate([weight_ref[0, slot] for slot in range(slots)], 1)
    )

    def times(left, right):
        return lax.dot_general(
            left, right, (((1,), (1,)), ((), ())), preferred_element_type=jnp.float32
        )

    applied = times(high, weight_high) + (times(high, weight_low) + times(low, weight_high))
    change = density_ref[...] * (applied - pieces[0])
    if scale is None:
        out_ref[0] = change
        at = 0
        for start in range(0, out_ref.shape[1], SIDE**3):
            for a, b in surface_runs():
                refs[-1][0, at : at + b - a, :] = out_ref[0, start + a : start + b, :]
                at += b - a
    else:
        out_ref[0] = refs[slots + 2][0] + scale * change


def collide(value, weights, columns, density, rest=None, scale=None):
    _, rows, width = value.shape
    blocks, slots, span, _ = weights.shape
    per = width // span

    def piece(slot):
        def index(b, column_ref):
            column = column_ref[b * slots + slot]
            return (column // per, 0, column % per)

        return pl.BlockSpec((1, rows, span), index)

    def result(count):
        return pl.BlockSpec((1, count, span), lambda b, column_ref: (b // per, 0, b % per))

    out_specs, out_shape = result(rows), jax.ShapeDtypeStruct(value.shape, jnp.float32)
    if rest is None:
        seen = rows // SIDE**3 * len(surface_nodes())
        out_specs = [out_specs, result(seen)]
        out_shape = [out_shape, jax.ShapeDtypeStruct((value.shape[0], seen, width), jnp.float32)]
    in_specs = [piece(slot) for slot in range(slots)]
    in_specs.append(pl.BlockSpec((1, slots, span, span), lambda b, column_ref: (b, 0, 0, 0)))
    in_specs.append(pl.BlockSpec((rows, span), lambda b, column_ref: (0, 0)))
    operands = [value] * slots + [weights, density]
    if rest is not None:
        in_specs.append(out_specs)
        operands.append(rest)
    return pl.pallas_call(
        functools.partial(collide_kernel, slots, scale),
        grid_spec=pltpu.PrefetchScalarGridSpec(
            num_scalar_prefetch=1, grid=(blocks,), in_specs=in_specs, out_specs=out_specs
        ),
        out_shape=out_shape,
        compiler_params=params(24),
        cost_estimate=cost(
            12 * rows * blocks * slots * span * span,
            4 * (value.size * (slots + 1 + (rest is not None)) + weights.size),
        ),
        name="collide",
    )(columns, *operands)


def surface_runs():
    runs = []
    for node in range(SIDE**3):
        index = (node // 16, node // 4 % 4, node % 4)
        if any(i in (0, SIDE - 1) for i in index):
            if runs and runs[-1][1] == node:
                runs[-1][1] = node + 1
            else:
                runs.append([node, node + 1])
    return runs


def surface_nodes():
    return [node for a, b in surface_runs() for node in range(a, b)]


def body(
    n_space,
    n_vel,
    distribution,
    inverse_jacobian,
    density,
    collision_blocks,
    block_columns,
    send_lists,
    exterior_faces,
):
    elements, nodes, width = distribution.shape
    owned = elements // n_vel
    rows = owned * nodes
    cap = send_lists.shape[2]
    local_faces = FACES * elements
    space_id = lax.axis_index("space")
    vel_id = lax.axis_index("vel")
    paired = n_space & (n_space - 1) == 0

    def partner(rank, step):
        return rank ^ step if paired else (rank + step) % n_space

    steps = range(1, n_space)
    send_rows = send_lists[0]
    send_ids = jnp.concatenate(
        [lax.dynamic_index_in_dim(send_rows, partner(space_id, step), 0, False) for step in steps]
    )
    lookup = exterior_faces.reshape(-1)
    source = (lookup - local_faces) // cap
    slot = (lookup - local_faces) % cap
    back = source ^ space_id if paired else (space_id - source) % n_space
    received = jnp.where(back == 0, 0, local_faces + (back - 1) * cap + slot)
    lookup = jnp.where(
        lookup < local_faces,
        lookup,
        jnp.where(
            lookup >= local_faces + n_space * cap, local_faces + (n_space - 1) * cap, received
        ),
    )

    jacobian = inverse_jacobian.reshape(-1)
    own_jacobian = lax.dynamic_slice_in_dim(jacobian, vel_id * owned * 9, owned * 9)
    own_density = lax.dynamic_slice_in_dim(density, vel_id * owned, owned).reshape(rows, 1)
    own_density = jnp.broadcast_to(own_density, (rows, collision_blocks.shape[2]))
    velocities = grid_velocities(0, n_vel * width).reshape(3, n_vel, width).transpose(1, 0, 2)
    velocity = grid_velocities(vel_id * width, width)
    columns = block_columns.reshape(-1)
    derivative = jnp.asarray(derivative_parts())
    lift = jnp.asarray(lift_parts())
    pack = jnp.asarray(pack_parts())
    spread = jnp.asarray(spread_parts())

    def exchange(value):
        return lax.all_to_all(value, "vel", split_axis=0, concat_axis=0, tiled=True)

    def neighbours(values, matrix, scale):
        table, *outgoing = faces(values, send_ids, n_space - 1, cap)
        incoming = jnp.concatenate(
            [
                lax.ppermute(out, "space", [(i, partner(i, step)) for i in range(n_space)])
                for step, out in zip(steps, outgoing)
            ]
        )
        return inflow(table, incoming, lookup, jacobian, velocity, matrix, scale, n_vel)

    value_own = exchange(distribution.reshape(n_vel, rows, width))
    flux = neighbours([distribution], pack, None)
    start = guess(distribution, flux, jacobian, velocity, derivative, spread)

    flux, value_own, start = lax.optimization_barrier((flux, value_own, start))
    flux_own = exchange(flux)
    change, seen = collide(value_own, collision_blocks, columns, own_density)

    seen, flux_own = lax.optimization_barrier((seen, flux_own))
    seen = exchange(seen)
    shape = (n_vel, owned, nodes, width)
    first, rest = stage(
        value_own.reshape(shape),
        flux_own,
        change.reshape(shape),
        own_jacobian,
        velocities,
        derivative,
        spread,
    )
    total = collide(
        first.reshape(n_vel, rows, width),
        collision_blocks,
        columns,
        own_density,
        rest.reshape(n_vel, rows, width),
        0.5 * TIME_STEP,
    )

    total, seen = lax.optimization_barrier((total, seen))
    total = exchange(total)
    seen = seen.reshape(elements, -1, width)
    outer = neighbours([start, seen], lift, 0.5 * TIME_STEP)
    return total.reshape(distribution.shape) + outer


def solution(mesh):
    in_specs = (
        P("space", None, "vel"),
        P("space", None, None),
        P("space", None),
        P(),
        P(),
        P("space", None, None),
        P("space", None),
    )
    out_specs = P("space", None, "vel")
    step = functools.partial(body, mesh.shape["space"], mesh.shape["vel"])
    return jax.shard_map(step, mesh=mesh, in_specs=in_specs, out_specs=out_specs, check_vma=False)
```

```python
import functools

import jax
import jax.numpy as jnp
import numpy as np
from jax import lax
from jax.experimental import pallas as pl
from jax.experimental.pallas import tpu as pltpu
from jax.sharding import PartitionSpec as P


VG = 16
SIDE = 4
FACES = 6
FACE_NODES = 16
LANES = 128

TIME_STEP = 0.03
LIFT_SCALE = 6.0


MIB = 1024 * 1024


def lagrange_derivative():
    points = np.array([-1.0, -1.0 / np.sqrt(5.0), 1.0 / np.sqrt(5.0), 1.0])
    barycentric = np.ones(4)
    for column in range(4):
        for second in range(4):
            if second != column:
                barycentric[column] = barycentric[column] / (points[column] - points[second])
    matrix = np.zeros((4, 4))
    for row_node in range(4):
        for col_node in range(4):
            if row_node != col_node:
                matrix[row_node, col_node] = (
                    barycentric[col_node]
                    / barycentric[row_node]
                    / (points[row_node] - points[col_node])
                )
        matrix[row_node, row_node] = -np.sum(matrix[row_node])
    return matrix


def derivative_parts():
    single = lagrange_derivative()
    identity = np.eye(4)
    stacked = np.concatenate(
        [
            np.kron(np.kron(single, identity), identity),
            np.kron(np.kron(identity, single), identity),
            np.kron(np.kron(identity, identity), single),
        ],
        0,
    ).astype(np.float32)
    high = stacked.astype(jnp.bfloat16)
    low = (stacked - high.astype(np.float32)).astype(jnp.bfloat16)
    return np.concatenate([high, high, low], 1)


def lift_parts():
    nodes = SIDE**3
    place = np.zeros((nodes, 3, 2, FACE_NODES), np.float32)
    for node in range(nodes):
        index = (node // 16, node // 4 % 4, node % 4)
        for direction in range(3):
            others = [index[d] for d in range(3) if d != direction]
            if index[direction] == 0:
                place[node, direction, 0, others[0] * 4 + others[1]] = 1.0
            if index[direction] == SIDE - 1:
                place[node, direction, 1, others[0] * 4 + others[1]] = 1.0
    place = place.reshape(nodes, 6 * FACE_NODES).astype(jnp.bfloat16)
    return np.concatenate([place, place], 1)


def shell():
    nodes = np.ndindex(SIDE, SIDE, SIDE)
    return [index for index in nodes if 0 in index]


SHELL = len(shell())
SHELL_MAIN = SHELL // 32 * 32
SHELL_ROWS = -(-SHELL // 8) * 8


def turned(index, flip):
    return tuple(SIDE - 1 - i if f else i for i, f in zip(index, flip))


def pack_parts():
    rows = {index: row for row, index in enumerate(shell())}
    pack = np.zeros((SHELL_ROWS, 3, 2, 2, FACE_NODES), np.float32)
    for direction in range(3):
        for first, second, a, b in np.ndindex(2, 2, SIDE, SIDE):
            where = list(turned((a, b), (first, second)))
            where.insert(direction, 0)
            pack[rows[tuple(where)], direction, first, second, a * SIDE + b] = 1.0
    pack = pack.reshape(SHELL_ROWS, -1).astype(jnp.bfloat16)
    return np.concatenate([pack, pack], 1)


def spread_parts():
    spread = np.zeros((SIDE, SIDE, SIDE, 2, 2, 2, SHELL_ROWS), np.float32)
    for flip in np.ndindex(2, 2, 2):
        for row, index in enumerate(shell()):
            spread[turned(index, flip) + flip + (row,)] = 1.0
    spread = spread.reshape(SIDE**3, -1).astype(jnp.bfloat16)
    return np.concatenate([spread, spread], 1)


def grid_velocities(first_id, amount):
    velocity_id = first_id + jnp.arange(amount, dtype=jnp.int32)
    components = [velocity_id // (VG * VG), velocity_id // VG % VG, velocity_id % VG]
    return jnp.stack(
        [3.0 * ((2.0 * component.astype(jnp.float32) + 1.0) / VG - 1.0) for component in components]
    )


def halves(value):
    high = value.astype(jnp.bfloat16)
    return high, (value - high.astype(jnp.float32)).astype(jnp.bfloat16)


def speeds_of(jacobian_ref, element, velocity):
    result = []
    for direction in range(3):
        base = element * 9 + direction * 3
        result.append(
            jacobian_ref[base] * velocity[0:1]
            + jacobian_ref[base + 1] * velocity[1:2]
            + jacobian_ref[base + 2] * velocity[2:3]
        )
    return result


def lifted(fluxes, speeds, lift):
    pieces = []
    for flux, speed in zip(fluxes, speeds):
        inward = speed > 0.0
        pieces.append(jnp.where(inward, flux, 0.0))
        pieces.append(jnp.where(inward, 0.0, flux))
    high, low = halves(jnp.concatenate(pieces, 0))
    return jnp.dot(lift, jnp.concatenate([high, low], 0), preferred_element_type=jnp.float32)


def signs(speeds):
    return [(jnp.where(s > 0.0, 1.0, 0.0), jnp.where(s > 0.0, 0.0, 1.0)) for s in speeds]


def packed(fluxes, speeds, pack):
    masks = signs(speeds)
    pieces = []
    for direction, flux in enumerate(fluxes):
        first, second = [masks[d] for d in range(3) if d != direction]
        pieces += [flux * (a * b) for a in first for b in second]
    high, low = halves(jnp.concatenate(pieces, 0))
    return jnp.dot(pack, jnp.concatenate([high, low], 0), preferred_element_type=jnp.float32)


def spread_out(rows, speeds, spread):
    masks = signs(speeds)
    pieces = [rows * (a * b * c) for a in masks[0] for b in masks[1] for c in masks[2]]
    high, low = halves(jnp.concatenate(pieces, 0))
    return jnp.dot(spread, jnp.concatenate([high, low], 0), preferred_element_type=jnp.float32)


def shell_rows(flux_ref, tail_ref, owned, element):
    for row in range(SHELL - SHELL_MAIN):
        at = owned * SHELL_MAIN + row * owned + element
        tail_ref[row : row + 1, :] = flux_ref[0, pl.ds(at, 1), :]
    for row in range(SHELL - SHELL_MAIN, tail_ref.shape[0]):
        tail_ref[row : row + 1, :] = jnp.zeros((1, tail_ref.shape[1]), jnp.float32)
    start = pl.multiple_of(element * SHELL_MAIN, SHELL_MAIN)
    return lambda lanes: jnp.concatenate(
        [flux_ref[0, pl.ds(start, SHELL_MAIN), lanes], tail_ref[:, lanes]], 0
    )


def own_flow(value, speeds, derivative):
    high, low = halves(value)
    slopes = jnp.dot(
        derivative, jnp.concatenate([high, low, high], 0), preferred_element_type=jnp.float32
    )
    node = lax.broadcasted_iota(jnp.int32, value.shape, 0)
    count = value.shape[0]
    total = None
    for direction in range(3):
        speed = speeds[direction]
        place = (node >> (4 - 2 * direction)) & 3
        side = jnp.where(speed > 0.0, 0, SIDE - 1)
        edge = jnp.where(place == side, LIFT_SCALE * jnp.abs(speed), 0.0)
        term = speed * slopes[direction * count : (direction + 1) * count] + edge * value
        total = term if total is None else total + term
    return -total


def lane_chunks(width):
    step = 2 * LANES if width % (2 * LANES) == 0 else LANES
    return [pl.ds(start, step) for start in range(0, width, step)]


def whole(space=pltpu.VMEM):
    return pl.BlockSpec(memory_space=space)


def params(mebibytes):
    return pltpu.CompilerParams(vmem_limit_bytes=mebibytes * MIB)


def cost(flops, moved):
    return pl.CostEstimate(flops=int(flops), bytes_accessed=int(moved), transcendentals=0)


def faces_kernel(cap, others, send_ref, *refs):
    value_ref = refs[0]
    change_ref = refs[1] if len(refs) > others + 2 else None
    table_ref, out_refs = refs[-1 - others], refs[len(refs) - others :]
    elements = value_ref.shape[0]
    surface = surface_nodes()

    def rows(element, start, stop):
        value = value_ref[element, start:stop, :]
        if change_ref is None:
            return value
        at = surface.index(start)
        return value + TIME_STEP * change_ref[element, at : at + stop - start, :]

    def build(element, carry):
        face = element * FACES
        table_ref[face] = rows(element, 0, 16)
        table_ref[face + 1] = rows(element, 48, 64)
        for i in range(SIDE):
            to = slice(4 * i, 4 * i + 4)
            table_ref[face + 2, to, :] = rows(element, 16 * i, 16 * i + 4)
            table_ref[face + 3, to, :] = rows(element, 16 * i + 12, 16 * i + 16)
        for m in range(FACE_NODES):
            to = slice(m, m + 1)
            table_ref[face + 4, to, :] = rows(element, 4 * m, 4 * m + 1)
            table_ref[face + 5, to, :] = rows(element, 4 * m + 3, 4 * m + 4)
        return carry

    lax.fori_loop(0, elements, build, 0)
    for number, out_ref in enumerate(out_refs):

        def pick(slot, carry, number=number, out_ref=out_ref):
            out_ref[slot] = table_ref[send_ref[number * cap + slot]]
            return carry

        lax.fori_loop(0, cap, pick, 0)


def faces(values, send_ids, others, cap):
    elements, _, width = values[0].shape
    out_shape = [jax.ShapeDtypeStruct((FACES * elements, FACE_NODES, width), jnp.float32)]
    out_shape += [jax.ShapeDtypeStruct((cap, FACE_NODES, width), jnp.float32)] * others
    moved = sum(value.size for value in values)
    moved += width * FACE_NODES * (FACES * elements + others * cap)
    return pl.pallas_call(
        functools.partial(faces_kernel, cap, others),
        out_shape=out_shape,
        in_specs=[whole(pltpu.SMEM)] + [whole()] * len(values),
        out_specs=[whole()] * (1 + others),
        compiler_params=params(44),
        cost_estimate=cost(0, 8 * moved),
        name="faces",
    )(send_ids, *values)


def inflow_kernel(scale, lookup_ref, jacobian_ref, velocity_ref, lift_ref, table_ref, in_ref, out_ref):
    local = table_ref.shape[0]
    remote = in_ref.shape[0]
    elements = local // FACES
    velocity = velocity_ref[...]

    def one(element, carry):
        speeds = speeds_of(jacobian_ref, element, velocity)
        fluxes = []
        for direction in range(3):
            traces = []
            for side in range(2):
                index = lookup_ref[element * FACES + 2 * direction + side]
                near = table_ref[jnp.minimum(index, local - 1)]
                far = in_ref[jnp.clip(index - local, 0, remote - 1)]
                far = jnp.where(index < local + remote, far, 0.0)
                traces.append(jnp.where(index < local, near, far))
            speed = speeds[direction]
            fluxes.append(
                (LIFT_SCALE * jnp.abs(speed)) * jnp.where(speed > 0.0, traces[0], traces[1])
            )
        if scale is None:
            owned = elements // out_ref.shape[0]
            owner, own = lax.div(element, owned), lax.rem(element, owned)
            rows = packed(fluxes, speeds, lift_ref[...])
            start = pl.multiple_of(own * SHELL_MAIN, SHELL_MAIN)
            out_ref[owner, pl.ds(start, SHELL_MAIN), :] = rows[:SHELL_MAIN]
            for row in range(SHELL_MAIN, SHELL):
                at = owned * SHELL_MAIN + (row - SHELL_MAIN) * owned + own
                out_ref[owner, pl.ds(at, 1), :] = rows[row : row + 1]
        else:
            out_ref[element] = scale * lifted(fluxes, speeds, lift_ref[...])
        return carry

    lax.fori_loop(0, elements, one, 0)


def inflow(table, incoming, lookup, jacobian, velocity, lift, scale, owners):
    width = table.shape[2]
    elements = table.shape[0] // FACES
    shape = (elements, SIDE**3, width)
    if scale is None:
        shape = (owners, elements // owners * SHELL, width)
    moved = table.size + incoming.size + np.prod(shape)
    return pl.pallas_call(
        functools.partial(inflow_kernel, scale),
        out_shape=jax.ShapeDtypeStruct(shape, jnp.float32),
        in_specs=[whole(pltpu.SMEM)] * 2 + [whole()] * 4,
        out_specs=whole(),
        compiler_params=params(36),
        cost_estimate=cost(0, 8 * moved),
        name="inflow",
    )(lookup, jacobian, velocity, lift, table, incoming)


def guess_kernel(
    owned, jacobian_ref, velocity_ref, derivative_ref, spread_ref, value_ref, flux_ref, out_ref, tail_ref
):
    element = pl.program_id(0)
    shell_of = shell_rows(flux_ref, tail_ref, owned, lax.rem(element, owned))
    for lanes in lane_chunks(value_ref.shape[2]):
        value = value_ref[0, :, lanes]
        speeds = speeds_of(jacobian_ref, element, velocity_ref[:, lanes])
        entering = spread_out(shell_of(lanes), speeds, spread_ref[...])
        flow = own_flow(value, speeds, derivative_ref[...]) + entering
        out_ref[0, :, lanes] = value + TIME_STEP * flow


def guess(value, flux, jacobian, velocity, derivative, spread):
    elements, nodes, width = value.shape
    owners, rows, _ = flux.shape
    owned = elements // owners
    return pl.pallas_call(
        functools.partial(guess_kernel, owned),
        grid=(elements,),
        out_shape=jax.ShapeDtypeStruct(value.shape, jnp.float32),
        in_specs=[
            whole(pltpu.SMEM),
            whole(),
            whole(),
            whole(),
            pl.BlockSpec((1, nodes, width), lambda e: (e, 0, 0)),
            pl.BlockSpec((1, rows, width), lambda e: (e // owned, 0, 0)),
        ],
        out_specs=pl.BlockSpec((1, nodes, width), lambda e: (e, 0, 0)),
        scratch_shapes=[pltpu.VMEM((SHELL_ROWS - SHELL_MAIN, width), jnp.float32)],
        compiler_params=params(16),
        cost_estimate=cost(2 * 256 * 192 * value.size // 64, 4 * (2 * value.size + flux.size)),
        name="guess",
    )(jacobian, velocity, derivative, spread, value, flux)


def stage_kernel(
    order_ref,
    jacobian_ref,
    velocity_ref,
    derivative_ref,
    spread_ref,
    value_ref,
    flux_ref,
    change_ref,
    first_ref,
    rest_ref,
    tail_ref,
):
    element = pl.program_id(1)
    shell_of = shell_rows(flux_ref, tail_ref, pl.num_programs(1), element)
    for lanes in lane_chunks(value_ref.shape[3]):
        value = value_ref[0, 0, :, lanes]
        speeds = speeds_of(jacobian_ref, element, velocity_ref[0, :, lanes])
        entering = spread_out(shell_of(lanes), speeds, spread_ref[...])
        flow = own_flow(value, speeds, derivative_ref[...]) + entering
        first = value + TIME_STEP * (flow + change_ref[0, 0, :, lanes])
        first_ref[0, 0, :, lanes] = first
        again = own_flow(first, speeds, derivative_ref[...])
        rest_ref[0, 0, :, lanes] = 0.5 * value + 0.5 * (first + TIME_STEP * again)


def stage(order, value, flux, change, jacobian, velocities, derivative, spread):
    chunks, elements, nodes, width = value.shape
    rows = flux.shape[1]
    block = pl.BlockSpec((1, 1, nodes, width), lambda c, e, order_ref: (order_ref[c], e, 0, 0))
    fixed = [
        pl.BlockSpec(part.shape, lambda c, e, order_ref: (0, 0)) for part in (derivative, spread)
    ]
    return pl.pallas_call(
        stage_kernel,
        grid_spec=pltpu.PrefetchScalarGridSpec(
            num_scalar_prefetch=1,
            grid=(chunks, elements),
            in_specs=[
                whole(pltpu.SMEM),
                pl.BlockSpec((1, 3, width), lambda c, e, order_ref: (order_ref[c], 0, 0)),
                *fixed,
                block,
                pl.BlockSpec((1, rows, width), lambda c, e, order_ref: (c, 0, 0)),
                block,
            ],
            out_specs=[block, block],
            scratch_shapes=[pltpu.VMEM((SHELL_ROWS - SHELL_MAIN, width), jnp.float32)],
        ),
        out_shape=[jax.ShapeDtypeStruct(value.shape, jnp.float32)] * 2,
        compiler_params=params(16),
        cost_estimate=cost(2 * 450 * 192 * value.size // 64, 4 * (4 * value.size + flux.size)),
        name="stage",
    )(order, jacobian, velocities, derivative, spread, value, flux, change)


def collide_kernel(slots, scale, column_ref, *refs):
    piece_refs = refs[:slots]
    weight_ref, density_ref = refs[slots : slots + 2]
    out_ref = refs[slots + 2 + (scale is not None)]
    pieces = [ref[0] for ref in piece_refs]
    high, low = halves(jnp.concatenate(pieces, 1))
    weight_high, weight_low = halves(
        jnp.concatenate([weight_ref[0, slot] for slot in range(slots)], 1)
    )

    def times(left, right):
        return lax.dot_general(
            left, right, (((1,), (1,)), ((), ())), preferred_element_type=jnp.float32
        )

    applied = times(high, weight_high) + (times(high, weight_low) + times(low, weight_high))
    change = density_ref[...] * (applied - pieces[0])
    if scale is None:
        out_ref[0] = change
        at = 0
        for start in range(0, out_ref.shape[1], SIDE**3):
            for a, b in surface_runs():
                refs[-1][0, at : at + b - a, :] = out_ref[0, start + a : start + b, :]
                at += b - a
    else:
        out_ref[0] = refs[slots + 2][0] + scale * change


def collide(value, weights, columns, density, rest=None, scale=None):
    _, rows, width = value.shape
    blocks, slots, span, _ = weights.shape
    per = width // span

    def piece(slot):
        def index(b, column_ref):
            column = column_ref[b * slots + slot]
            return (column // per, 0, column % per)

        return pl.BlockSpec((1, rows, span), index)

    def result(count):
        return pl.BlockSpec((1, count, span), lambda b, column_ref: (b // per, 0, b % per))

    out_specs, out_shape = result(rows), jax.ShapeDtypeStruct(value.shape, jnp.float32)
    if rest is None:
        seen = rows // SIDE**3 * len(surface_nodes())
        out_specs = [out_specs, result(seen)]
        out_shape = [out_shape, jax.ShapeDtypeStruct((value.shape[0], seen, width), jnp.float32)]
    in_specs = [piece(slot) for slot in range(slots)]
    in_specs.append(pl.BlockSpec((1, slots, span, span), lambda b, column_ref: (b, 0, 0, 0)))
    in_specs.append(pl.BlockSpec((rows, span), lambda b, column_ref: (0, 0)))
    operands = [value] * slots + [weights, density]
    if rest is not None:
        in_specs.append(out_specs)
        operands.append(rest)
    return pl.pallas_call(
        functools.partial(collide_kernel, slots, scale),
        grid_spec=pltpu.PrefetchScalarGridSpec(
            num_scalar_prefetch=1, grid=(blocks,), in_specs=in_specs, out_specs=out_specs
        ),
        out_shape=out_shape,
        compiler_params=params(24),
        cost_estimate=cost(
            12 * rows * blocks * slots * span * span,
            4 * (value.size * (slots + 1 + (rest is not None)) + weights.size),
        ),
        name="collide",
    )(columns, *operands)


def surface_runs():
    runs = []
    for node in range(SIDE**3):
        index = (node // 16, node // 4 % 4, node % 4)
        if any(i in (0, SIDE - 1) for i in index):
            if runs and runs[-1][1] == node:
                runs[-1][1] = node + 1
            else:
                runs.append([node, node + 1])
    return runs


def surface_nodes():
    return [node for a, b in surface_runs() for node in range(a, b)]


def after(value, other):
    return lax.optimization_barrier((value, other))[0]


def body(
    n_space,
    n_vel,
    distribution,
    inverse_jacobian,
    density,
    collision_blocks,
    block_columns,
    send_lists,
    exterior_faces,
):
    elements, nodes, width = distribution.shape
    owned = elements // n_vel
    rows = owned * nodes
    cap = send_lists.shape[2]
    local_faces = FACES * elements
    space_id = lax.axis_index("space")
    vel_id = lax.axis_index("vel")
    paired = n_space & (n_space - 1) == 0

    def partner(rank, step):
        return rank ^ step if paired else (rank + step) % n_space

    vel_paired = n_vel & (n_vel - 1) == 0

    def to_peer(rank, step):
        return rank ^ step if vel_paired else (rank + step) % n_vel

    def from_peer(rank, step):
        return rank ^ step if vel_paired else (rank - step) % n_vel

    def hand_over(value):
        blocks = [
            lax.dynamic_index_in_dim(value, to_peer(vel_id, step), 0, False) for step in range(n_vel)
        ]
        blocks = list(lax.optimization_barrier(blocks))
        for step in range(1, n_vel):
            pairs = [(i, to_peer(i, step)) for i in range(n_vel)]
            blocks[step] = lax.ppermute(blocks[step], "vel", pairs)
        return blocks

    steps = range(1, n_space)
    send_rows = send_lists[0]
    send_ids = jnp.concatenate(
        [lax.dynamic_index_in_dim(send_rows, partner(space_id, step), 0, False) for step in steps]
    )
    lookup = exterior_faces.reshape(-1)
    source = (lookup - local_faces) // cap
    slot = (lookup - local_faces) % cap
    back = source ^ space_id if paired else (space_id - source) % n_space
    received = jnp.where(back == 0, 0, local_faces + (back - 1) * cap + slot)
    lookup = jnp.where(
        lookup < local_faces,
        lookup,
        jnp.where(
            lookup >= local_faces + n_space * cap, local_faces + (n_space - 1) * cap, received
        ),
    )

    jacobian = inverse_jacobian.reshape(-1)
    own_jacobian = lax.dynamic_slice_in_dim(jacobian, vel_id * owned * 9, owned * 9)
    own_density = lax.dynamic_slice_in_dim(density, vel_id * owned, owned).reshape(rows, 1)
    own_density = jnp.broadcast_to(own_density, (rows, collision_blocks.shape[2]))
    velocities = grid_velocities(0, n_vel * width).reshape(3, n_vel, width).transpose(1, 0, 2)
    velocity = grid_velocities(vel_id * width, width)
    columns = block_columns.reshape(-1)
    derivative = jnp.asarray(derivative_parts())
    lift = jnp.asarray(lift_parts())
    pack = jnp.asarray(pack_parts())
    spread = jnp.asarray(spread_parts())

    def exchange(value):
        return lax.all_to_all(value, "vel", split_axis=0, concat_axis=0, tiled=True)

    def neighbours(values, matrix, scale):
        table, *outgoing = faces(values, send_ids, n_space - 1, cap)
        incoming = jnp.concatenate(
            [
                lax.ppermute(out, "space", [(i, partner(i, step)) for i in range(n_space)])
                for step, out in zip(steps, outgoing)
            ]
        )
        return inflow(table, incoming, lookup, jacobian, velocity, matrix, scale, n_vel)

    value_own = exchange(distribution.reshape(n_vel, rows, width))
    flux = neighbours([distribution], pack, None)
    start = guess(distribution, flux, jacobian, velocity, derivative, spread)

    flux, start = lax.optimization_barrier((flux, start))
    flux_own = hand_over(flux)
    value_own = after(value_own, start)
    change, seen = collide(value_own, collision_blocks, columns, own_density)

    seen = exchange(seen)
    flux_own = jnp.stack(flux_own)
    shape = (n_vel, owned, nodes, width)
    first, rest = stage(
        jnp.stack([from_peer(vel_id, step) for step in range(n_vel)]),
        value_own.reshape(shape),
        flux_own,
        change.reshape(shape),
        own_jacobian,
        velocities,
        derivative,
        spread,
    )
    total = collide(
        first.reshape(n_vel, rows, width),
        collision_blocks,
        columns,
        own_density,
        rest.reshape(n_vel, rows, width),
        0.5 * TIME_STEP,
    )

    totals = hand_over(total)
    seen = after(seen, total)
    seen = seen.reshape(elements, -1, width)
    outer = neighbours([start, seen], lift, 0.5 * TIME_STEP)
    result = outer.reshape(n_vel, rows, width)
    for step, block in enumerate(totals):
        at = from_peer(vel_id, step)
        block = block + lax.dynamic_index_in_dim(result, at, 0, False)
        result = lax.dynamic_update_index_in_dim(result, block, at, 0)
    return result.reshape(distribution.shape)


def solution(mesh):
    in_specs = (
        P("space", None, "vel"),
        P("space", None, None),
        P("space", None),
        P(),
        P(),
        P("space", None, None),
        P("space", None),
    )
    out_specs = P("space", None, "vel")

    def step(*arguments):
        return body(mesh.shape["space"], mesh.shape["vel"], *arguments)

    return jax.shard_map(
        step, mesh=mesh, in_specs=in_specs, out_specs=out_specs, check_vma=False
    )
```

```python
import functools

import jax
import jax.numpy as jnp
import numpy as np
from jax import lax
from jax.experimental import pallas as pl
from jax.experimental.pallas import tpu as pltpu
from jax.sharding import PartitionSpec as P


VG = 16
SIDE = 4
FACES = 6
FACE_NODES = 16
LANES = 128

TIME_STEP = 0.03
LIFT_SCALE = 6.0


MIB = 1024 * 1024


def lagrange_derivative():
    points = np.array([-1.0, -1.0 / np.sqrt(5.0), 1.0 / np.sqrt(5.0), 1.0])
    barycentric = np.ones(4)
    for column in range(4):
        for second in range(4):
            if second != column:
                barycentric[column] = barycentric[column] / (points[column] - points[second])
    matrix = np.zeros((4, 4))
    for row_node in range(4):
        for col_node in range(4):
            if row_node != col_node:
                matrix[row_node, col_node] = (
                    barycentric[col_node]
                    / barycentric[row_node]
                    / (points[row_node] - points[col_node])
                )
        matrix[row_node, row_node] = -np.sum(matrix[row_node])
    return matrix


def derivative_parts():
    single = lagrange_derivative()
    identity = np.eye(4)
    stacked = np.concatenate(
        [
            np.kron(np.kron(single, identity), identity),
            np.kron(np.kron(identity, single), identity),
            np.kron(np.kron(identity, identity), single),
        ],
        0,
    ).astype(np.float32)
    high = stacked.astype(jnp.bfloat16)
    low = (stacked - high.astype(np.float32)).astype(jnp.bfloat16)
    return np.concatenate([high, high, low], 1)


def lift_parts():
    nodes = SIDE**3
    place = np.zeros((nodes, 3, 2, FACE_NODES), np.float32)
    for node in range(nodes):
        index = (node // 16, node // 4 % 4, node % 4)
        for direction in range(3):
            others = [index[d] for d in range(3) if d != direction]
            if index[direction] == 0:
                place[node, direction, 0, others[0] * 4 + others[1]] = 1.0
            if index[direction] == SIDE - 1:
                place[node, direction, 1, others[0] * 4 + others[1]] = 1.0
    place = place.reshape(nodes, 6 * FACE_NODES).astype(jnp.bfloat16)
    return np.concatenate([place, place], 1)


def shell():
    nodes = np.ndindex(SIDE, SIDE, SIDE)
    return [index for index in nodes if 0 in index]


SHELL = len(shell())
SHELL_MAIN = SHELL // 32 * 32
SHELL_ROWS = -(-SHELL // 8) * 8


def turned(index, flip):
    return tuple(SIDE - 1 - i if f else i for i, f in zip(index, flip))


def pack_parts():
    rows = {index: row for row, index in enumerate(shell())}
    pack = np.zeros((SHELL_ROWS, 3, 2, 2, FACE_NODES), np.float32)
    for direction in range(3):
        for first, second, a, b in np.ndindex(2, 2, SIDE, SIDE):
            where = list(turned((a, b), (first, second)))
            where.insert(direction, 0)
            pack[rows[tuple(where)], direction, first, second, a * SIDE + b] = 1.0
    pack = pack.reshape(SHELL_ROWS, -1).astype(jnp.bfloat16)
    return np.concatenate([pack, pack], 1)


def spread_parts():
    spread = np.zeros((SIDE, SIDE, SIDE, 2, 2, 2, SHELL_ROWS), np.float32)
    for flip in np.ndindex(2, 2, 2):
        for row, index in enumerate(shell()):
            spread[turned(index, flip) + flip + (row,)] = 1.0
    spread = spread.reshape(SIDE**3, -1).astype(jnp.bfloat16)
    return np.concatenate([spread, spread], 1)


def grid_velocities(first_id, amount):
    velocity_id = first_id + jnp.arange(amount, dtype=jnp.int32)
    components = [velocity_id // (VG * VG), velocity_id // VG % VG, velocity_id % VG]
    return jnp.stack(
        [3.0 * ((2.0 * component.astype(jnp.float32) + 1.0) / VG - 1.0) for component in components]
    )


def halves(value):
    high = value.astype(jnp.bfloat16)
    return high, (value - high.astype(jnp.float32)).astype(jnp.bfloat16)


def speeds_of(jacobian_ref, element, velocity):
    result = []
    for direction in range(3):
        base = element * 9 + direction * 3
        result.append(
            jacobian_ref[base] * velocity[0:1]
            + jacobian_ref[base + 1] * velocity[1:2]
            + jacobian_ref[base + 2] * velocity[2:3]
        )
    return result


def lifted(fluxes, speeds, lift):
    pieces = []
    for flux, speed in zip(fluxes, speeds):
        inward = speed > 0.0
        pieces.append(jnp.where(inward, flux, 0.0))
        pieces.append(jnp.where(inward, 0.0, flux))
    high, low = halves(jnp.concatenate(pieces, 0))
    return jnp.dot(lift, jnp.concatenate([high, low], 0), preferred_element_type=jnp.float32)


def signs(speeds):
    return [(jnp.where(s > 0.0, 1.0, 0.0), jnp.where(s > 0.0, 0.0, 1.0)) for s in speeds]


def packed(fluxes, speeds, pack):
    masks = signs(speeds)
    pieces = []
    for direction, flux in enumerate(fluxes):
        first, second = [masks[d] for d in range(3) if d != direction]
        pieces += [flux * (a * b) for a in first for b in second]
    high, low = halves(jnp.concatenate(pieces, 0))
    return jnp.dot(pack, jnp.concatenate([high, low], 0), preferred_element_type=jnp.float32)


def spread_out(rows, speeds, spread):
    masks = signs(speeds)
    pieces = [rows * (a * b * c) for a in masks[0] for b in masks[1] for c in masks[2]]
    high, low = halves(jnp.concatenate(pieces, 0))
    return jnp.dot(spread, jnp.concatenate([high, low], 0), preferred_element_type=jnp.float32)


def shell_rows(flux_ref, tail_ref, owned, element):
    for row in range(SHELL - SHELL_MAIN):
        at = owned * SHELL_MAIN + row * owned + element
        tail_ref[row : row + 1, :] = flux_ref[0, pl.ds(at, 1), :]
    for row in range(SHELL - SHELL_MAIN, tail_ref.shape[0]):
        tail_ref[row : row + 1, :] = jnp.zeros((1, tail_ref.shape[1]), jnp.float32)
    start = pl.multiple_of(element * SHELL_MAIN, SHELL_MAIN)
    return lambda lanes: jnp.concatenate(
        [flux_ref[0, pl.ds(start, SHELL_MAIN), lanes], tail_ref[:, lanes]], 0
    )


def own_flow(value, speeds, derivative):
    high, low = halves(value)
    slopes = jnp.dot(
        derivative, jnp.concatenate([high, low, high], 0), preferred_element_type=jnp.float32
    )
    node = lax.broadcasted_iota(jnp.int32, value.shape, 0)
    count = value.shape[0]
    total = None
    for direction in range(3):
        speed = speeds[direction]
        place = (node >> (4 - 2 * direction)) & 3
        side = jnp.where(speed > 0.0, 0, SIDE - 1)
        edge = jnp.where(place == side, LIFT_SCALE * jnp.abs(speed), 0.0)
        term = speed * slopes[direction * count : (direction + 1) * count] + edge * value
        total = term if total is None else total + term
    return -total


def lane_chunks(width):
    step = 2 * LANES if width % (2 * LANES) == 0 else LANES
    return [pl.ds(start, step) for start in range(0, width, step)]


def whole(space=pltpu.VMEM):
    return pl.BlockSpec(memory_space=space)


def params(mebibytes):
    return pltpu.CompilerParams(vmem_limit_bytes=mebibytes * MIB)


def cost(flops, moved):
    return pl.CostEstimate(flops=int(flops), bytes_accessed=int(moved), transcendentals=0)


def faces_kernel(cap, others, parts, send_ref, *refs):
    value_refs = refs[: len(refs) - 1 - others]
    table_ref, out_refs = refs[-1 - others], refs[len(refs) - others :]
    surface = surface_nodes()
    per_part = len(value_refs) // parts
    base = 0
    for part in range(parts):
        value_ref, *change_refs = value_refs[part * per_part : (part + 1) * per_part]

        def build(element, carry, value_ref=value_ref, change_refs=change_refs, base=base):
            def rows(start, stop):
                value = value_ref[element, start:stop, :]
                if not change_refs:
                    return value
                at = surface.index(start)
                return value + TIME_STEP * change_refs[0][element, at : at + stop - start, :]

            face = (base + element) * FACES
            table_ref[face] = rows(0, 16)
            table_ref[face + 1] = rows(48, 64)
            for i in range(SIDE):
                to = slice(4 * i, 4 * i + 4)
                table_ref[face + 2, to, :] = rows(16 * i, 16 * i + 4)
                table_ref[face + 3, to, :] = rows(16 * i + 12, 16 * i + 16)
            for m in range(FACE_NODES):
                to = slice(m, m + 1)
                table_ref[face + 4, to, :] = rows(4 * m, 4 * m + 1)
                table_ref[face + 5, to, :] = rows(4 * m + 3, 4 * m + 4)
            return carry

        lax.fori_loop(0, value_ref.shape[0], build, 0)
        base += value_ref.shape[0]
    for number, out_ref in enumerate(out_refs):

        def pick(slot, carry, number=number, out_ref=out_ref):
            out_ref[slot] = table_ref[send_ref[number * cap + slot]]
            return carry

        lax.fori_loop(0, cap, pick, 0)


def faces(parts, send_ids, others, cap):
    elements = sum(part[0].shape[0] for part in parts)
    width = parts[0][0].shape[2]
    values = [value for part in parts for value in part]
    out_shape = [jax.ShapeDtypeStruct((FACES * elements, FACE_NODES, width), jnp.float32)]
    out_shape += [jax.ShapeDtypeStruct((cap, FACE_NODES, width), jnp.float32)] * others
    moved = sum(value.size for value in values)
    moved += width * FACE_NODES * (FACES * elements + others * cap)
    return pl.pallas_call(
        functools.partial(faces_kernel, cap, others, len(parts)),
        out_shape=out_shape,
        in_specs=[whole(pltpu.SMEM)] + [whole()] * len(values),
        out_specs=[whole()] * (1 + others),
        compiler_params=params(44),
        cost_estimate=cost(0, 8 * moved),
        name="faces",
    )(send_ids, *values)


def inflow_kernel(
    scale, plan, lookup_ref, jacobian_ref, velocity_ref, lift_ref, table_ref, in_ref, *out_refs
):
    local = table_ref.shape[0]
    remote = in_ref.shape[0]
    elements = local // FACES
    velocity = velocity_ref[...]

    def one(element, carry, out_ref, base, owned):
        speeds = speeds_of(jacobian_ref, element, velocity)
        fluxes = []
        for direction in range(3):
            traces = []
            for side in range(2):
                index = lookup_ref[element * FACES + 2 * direction + side]
                near = table_ref[jnp.minimum(index, local - 1)]
                far = in_ref[jnp.clip(index - local, 0, remote - 1)]
                far = jnp.where(index < local + remote, far, 0.0)
                traces.append(jnp.where(index < local, near, far))
            speed = speeds[direction]
            fluxes.append(
                (LIFT_SCALE * jnp.abs(speed)) * jnp.where(speed > 0.0, traces[0], traces[1])
            )
        if scale is None:
            owner, own = lax.div(element - base, owned), lax.rem(element - base, owned)
            rows = packed(fluxes, speeds, lift_ref[...])
            start = pl.multiple_of(own * SHELL_MAIN, SHELL_MAIN)
            out_ref[owner, pl.ds(start, SHELL_MAIN), :] = rows[:SHELL_MAIN]
            for row in range(SHELL_MAIN, SHELL):
                at = owned * SHELL_MAIN + (row - SHELL_MAIN) * owned + own
                out_ref[owner, pl.ds(at, 1), :] = rows[row : row + 1]
        else:
            out_ref[element] = scale * lifted(fluxes, speeds, lift_ref[...])
        return carry

    if scale is None:
        base = 0
        for (owners, owned), out_ref in zip(plan, out_refs):
            part = functools.partial(one, out_ref=out_ref, base=base, owned=owned)
            lax.fori_loop(base, base + owners * owned, part, 0)
            base += owners * owned
    else:
        part = functools.partial(one, out_ref=out_refs[0], base=0, owned=elements)
        lax.fori_loop(0, elements, part, 0)


def inflow(table, incoming, lookup, jacobian, velocity, lift, scale, plan):
    width = table.shape[2]
    elements = table.shape[0] // FACES
    shapes = [(elements, SIDE**3, width)]
    if scale is None:
        shapes = [(owners, owned * SHELL, width) for owners, owned in plan]
    moved = table.size + incoming.size + sum(np.prod(shape) for shape in shapes)
    return pl.pallas_call(
        functools.partial(inflow_kernel, scale, plan),
        out_shape=[jax.ShapeDtypeStruct(shape, jnp.float32) for shape in shapes],
        in_specs=[whole(pltpu.SMEM)] * 2 + [whole()] * 4,
        out_specs=[whole()] * len(shapes),
        compiler_params=params(36),
        cost_estimate=cost(0, 8 * moved),
        name="inflow",
    )(lookup, jacobian, velocity, lift, table, incoming)


def guess_kernel(
    base,
    owned,
    jacobian_ref,
    velocity_ref,
    derivative_ref,
    spread_ref,
    value_ref,
    flux_ref,
    out_ref,
    tail_ref,
):
    element = base + pl.program_id(0)
    shell_of = shell_rows(flux_ref, tail_ref, owned, lax.rem(pl.program_id(0), owned))
    for lanes in lane_chunks(value_ref.shape[2]):
        value = value_ref[0, :, lanes]
        speeds = speeds_of(jacobian_ref, element, velocity_ref[:, lanes])
        entering = spread_out(shell_of(lanes), speeds, spread_ref[...])
        flow = own_flow(value, speeds, derivative_ref[...]) + entering
        out_ref[0, :, lanes] = value + TIME_STEP * flow


def guess(base, owned, value, flux, jacobian, velocity, derivative, spread):
    _, nodes, width = value.shape
    owners, rows, _ = flux.shape
    elements = owners * owned
    size = elements * nodes * width
    return pl.pallas_call(
        functools.partial(guess_kernel, base, owned),
        grid=(elements,),
        out_shape=jax.ShapeDtypeStruct((elements, nodes, width), jnp.float32),
        in_specs=[
            whole(pltpu.SMEM),
            whole(),
            whole(),
            whole(),
            pl.BlockSpec((1, nodes, width), lambda e: (base + e, 0, 0)),
            pl.BlockSpec((1, rows, width), lambda e: (e // owned, 0, 0)),
        ],
        out_specs=pl.BlockSpec((1, nodes, width), lambda e: (e, 0, 0)),
        scratch_shapes=[pltpu.VMEM((SHELL_ROWS - SHELL_MAIN, width), jnp.float32)],
        compiler_params=params(16),
        cost_estimate=cost(2 * 256 * 192 * size // 64, 4 * (2 * size + flux.size)),
        name="guess",
    )(jacobian, velocity, derivative, spread, value, flux)


def stage_kernel(
    jacobian_ref,
    velocity_ref,
    derivative_ref,
    spread_ref,
    value_ref,
    flux_ref,
    change_ref,
    first_ref,
    rest_ref,
    tail_ref,
):
    element = pl.program_id(1)
    shell_of = shell_rows(flux_ref, tail_ref, pl.num_programs(1), element)
    for lanes in lane_chunks(value_ref.shape[3]):
        value = value_ref[0, 0, :, lanes]
        speeds = speeds_of(jacobian_ref, element, velocity_ref[0, :, lanes])
        entering = spread_out(shell_of(lanes), speeds, spread_ref[...])
        flow = own_flow(value, speeds, derivative_ref[...]) + entering
        first = value + TIME_STEP * (flow + change_ref[0, 0, :, lanes])
        first_ref[0, 0, :, lanes] = first
        again = own_flow(first, speeds, derivative_ref[...])
        rest_ref[0, 0, :, lanes] = 0.5 * value + 0.5 * (first + TIME_STEP * again)


def stage(value, flux, change, jacobian, velocities, derivative, spread):
    chunks, elements, nodes, width = value.shape
    rows = flux.shape[1]
    block = pl.BlockSpec((1, 1, nodes, width), lambda c, e: (c, e, 0, 0))
    return pl.pallas_call(
        stage_kernel,
        grid=(chunks, elements),
        out_shape=[jax.ShapeDtypeStruct(value.shape, jnp.float32)] * 2,
        in_specs=[
            whole(pltpu.SMEM),
            pl.BlockSpec((1, 3, width), lambda c, e: (c, 0, 0)),
            whole(),
            whole(),
            block,
            pl.BlockSpec((1, rows, width), lambda c, e: (c, 0, 0)),
            block,
        ],
        out_specs=[block, block],
        scratch_shapes=[pltpu.VMEM((SHELL_ROWS - SHELL_MAIN, width), jnp.float32)],
        compiler_params=params(16),
        cost_estimate=cost(2 * 450 * 192 * value.size // 64, 4 * (4 * value.size + flux.size)),
        name="stage",
    )(jacobian, velocities, derivative, spread, value, flux, change)


def collide_kernel(slots, scale, column_ref, base_ref, *refs):
    piece_refs = refs[:slots]
    weight_ref, density_ref = refs[slots : slots + 2]
    out_ref = refs[slots + 2 + (scale is not None)]
    pieces = [ref[0] for ref in piece_refs]
    high, low = halves(jnp.concatenate(pieces, 1))
    weight_high, weight_low = halves(
        jnp.concatenate([weight_ref[0, slot] for slot in range(slots)], 1)
    )

    def times(left, right):
        return lax.dot_general(
            left, right, (((1,), (1,)), ((), ())), preferred_element_type=jnp.float32
        )

    applied = times(high, weight_high) + (times(high, weight_low) + times(low, weight_high))
    change = density_ref[...] * (applied - pieces[0])
    if scale is None:
        out_ref[0] = change
        at = 0
        for start in range(0, out_ref.shape[1], SIDE**3):
            for a, b in surface_runs():
                refs[-1][0, at : at + b - a, :] = out_ref[0, start + a : start + b, :]
                at += b - a
    else:
        out_ref[0] = refs[slots + 2][0] + scale * change


def collide(value, weights, columns, density, base=None, chunks=None, rest=None, scale=None):
    _, rows, width = value.shape
    blocks, slots, span, _ = weights.shape
    per = width // span
    chunks = blocks // per if chunks is None else chunks
    base = jnp.zeros((1,), jnp.int32) if base is None else base

    def piece(slot):
        def index(t, column_ref, base_ref):
            column = column_ref[(base_ref[0] + t) * slots + slot]
            return (column // per, 0, column % per)

        return pl.BlockSpec((1, rows, span), index)

    def result(count):
        return pl.BlockSpec(
            (1, count, span), lambda t, column_ref, base_ref: (t // per, 0, t % per)
        )

    in_specs = [piece(slot) for slot in range(slots)]
    in_specs.append(
        pl.BlockSpec(
            (1, slots, span, span), lambda t, column_ref, base_ref: (base_ref[0] + t, 0, 0, 0)
        )
    )
    in_specs.append(pl.BlockSpec((rows, span), lambda t, column_ref, base_ref: (0, 0)))
    operands = [value] * slots + [weights, density]
    out_specs = result(rows)
    out_shape = jax.ShapeDtypeStruct((chunks, rows, width), jnp.float32)
    if rest is None:
        seen = rows // SIDE**3 * len(surface_nodes())
        out_specs = [out_specs, result(seen)]
        out_shape = [out_shape, jax.ShapeDtypeStruct((chunks, seen, width), jnp.float32)]
    else:
        in_specs.append(
            pl.BlockSpec(
                (1, rows, span),
                lambda t, column_ref, base_ref: (
                    (base_ref[0] + t) // per,
                    0,
                    (base_ref[0] + t) % per,
                ),
            )
        )
        operands.append(rest)
    return pl.pallas_call(
        functools.partial(collide_kernel, slots, scale),
        grid_spec=pltpu.PrefetchScalarGridSpec(
            num_scalar_prefetch=2, grid=(chunks * per,), in_specs=in_specs, out_specs=out_specs
        ),
        out_shape=out_shape,
        compiler_params=params(24),
        cost_estimate=cost(
            12 * rows * chunks * per * slots * span * span,
            4 * (chunks * per * rows * span * (slots + 1) + weights.size),
        ),
        name="collide",
    )(columns, base, *operands)


def surface_runs():
    runs = []
    for node in range(SIDE**3):
        index = (node // 16, node // 4 % 4, node % 4)
        if any(i in (0, SIDE - 1) for i in index):
            if runs and runs[-1][1] == node:
                runs[-1][1] = node + 1
            else:
                runs.append([node, node + 1])
    return runs


def surface_nodes():
    return [node for a, b in surface_runs() for node in range(a, b)]


def after(value, other):
    return lax.optimization_barrier((value, other))[0]


def all_after(values, *others):
    return lax.optimization_barrier([*values, *others])[: len(values)]


def body(
    n_space,
    n_vel,
    distribution,
    inverse_jacobian,
    density,
    collision_blocks,
    block_columns,
    send_lists,
    exterior_faces,
):
    elements, nodes, width = distribution.shape
    half = n_vel // 2
    single_owned = elements * 5 // 8 // n_vel
    single = single_owned * n_vel
    shared_owned = (elements - single) // half
    assert n_vel & (n_vel - 1) == 0 and shared_owned * half == elements - single
    plan = ((n_vel, single_owned), (half, shared_owned))
    cap = send_lists.shape[2]
    local_faces = FACES * elements
    space_id = lax.axis_index("space")
    vel_id = lax.axis_index("vel")
    paired = n_space & (n_space - 1) == 0

    def partner(rank, step):
        return rank ^ step if paired else (rank + step) % n_space

    def hand_over(block_of, steps):
        blocks = list(lax.optimization_barrier([block_of(vel_id ^ step) for step in range(steps)]))
        for step in range(1, steps):
            pairs = [(i, i ^ step) for i in range(n_vel)]
            blocks[step] = lax.ppermute(blocks[step], "vel", pairs)
        return blocks

    def among(value, count):
        return lambda peer: lax.dynamic_index_in_dim(value, peer & (count - 1), 0, False)

    def in_order(blocks):
        count = len(blocks)
        result = jnp.zeros((count,) + blocks[0].shape, jnp.float32)
        for step, block in enumerate(blocks):
            at = (vel_id ^ step) & (count - 1)
            result = lax.dynamic_update_index_in_dim(result, block, at, 0)
        return result

    steps = range(1, n_space)
    send_rows = send_lists[0]
    send_ids = jnp.concatenate(
        [lax.dynamic_index_in_dim(send_rows, partner(space_id, step), 0, False) for step in steps]
    )
    lookup = exterior_faces.reshape(-1)
    source = (lookup - local_faces) // cap
    slot = (lookup - local_faces) % cap
    back = source ^ space_id if paired else (space_id - source) % n_space
    received = jnp.where(back == 0, 0, local_faces + (back - 1) * cap + slot)
    lookup = jnp.where(
        lookup < local_faces,
        lookup,
        jnp.where(
            lookup >= local_faces + n_space * cap, local_faces + (n_space - 1) * cap, received
        ),
    )

    jacobian = inverse_jacobian.reshape(-1)
    span = collision_blocks.shape[2]

    def owned_part(first, owned):
        rows = lax.dynamic_slice_in_dim(density, first, owned).reshape(-1, 1)
        return (
            lax.dynamic_slice_in_dim(jacobian, first * 9, owned * 9),
            jnp.broadcast_to(rows, (owned * nodes, span)),
        )

    single_jacobian, single_density = owned_part(vel_id * single_owned, single_owned)
    shared_jacobian, shared_density = owned_part(
        single + (vel_id & (half - 1)) * shared_owned, shared_owned
    )
    velocities = grid_velocities(0, n_vel * width).reshape(3, n_vel, width).transpose(1, 0, 2)
    velocity = grid_velocities(vel_id * width, width)
    columns = block_columns.reshape(-1)
    derivative = jnp.asarray(derivative_parts())
    lift = jnp.asarray(lift_parts())
    pack = jnp.asarray(pack_parts())
    spread = jnp.asarray(spread_parts())

    def exchange(value):
        return lax.all_to_all(value, "vel", split_axis=0, concat_axis=0, tiled=True)

    def cut_traces(parts):
        table, *outgoing = faces(parts, send_ids, n_space - 1, cap)
        incoming = [
            lax.ppermute(out, "space", [(i, partner(i, step)) for i in range(n_space)])
            for step, out in zip(steps, outgoing)
        ]
        return table, incoming

    def enter(table, incoming, matrix, scale):
        incoming = jnp.concatenate(incoming)
        return inflow(table, incoming, lookup, jacobian, velocity, matrix, scale, plan)

    def stage_of(value, flux, change, own_jacobian):
        shape = (n_vel, -1, nodes, width)
        first, rest = stage(
            value.reshape(shape),
            flux,
            change.reshape(shape),
            own_jacobian,
            velocities,
            derivative,
            spread,
        )
        return first.reshape(value.shape), rest.reshape(value.shape)

    collision = functools.partial(collide, weights=collision_blocks, columns=columns)

    value = exchange(distribution[:single].reshape(n_vel, -1, width))
    table, incoming = cut_traces([(distribution,)])
    (source,) = all_after([distribution], *incoming)

    def shared_block(peer):
        start = single + (peer & (half - 1)) * shared_owned
        return lax.dynamic_slice_in_dim(source, start, shared_owned).reshape(-1, width)

    shared = hand_over(shared_block, n_vel)
    flux_single, flux_shared = enter(table, incoming, pack, None)
    wave = (jacobian, velocity, derivative, spread)
    start_shared = guess(single, shared_owned, distribution, flux_shared, *wave)
    start_single = guess(0, single_owned, distribution, flux_single, *wave)
    flux_single = hand_over(among(after(flux_single, start_shared), n_vel), n_vel)

    value = after(value, start_single)
    change, seen = collision(value, density=single_density)
    seen = exchange(all_after([seen], *flux_single)[0])
    flux_single = in_order(all_after(flux_single, change))
    first, rest = stage_of(value, flux_single, change, single_jacobian)
    total = collision(first, density=single_density, rest=rest, scale=0.5 * TIME_STEP)

    flux_shared = hand_over(among(after(flux_shared, total), half), n_vel)
    shared = in_order(all_after(shared, total))
    change_shared, seen_shared = collision(shared, density=shared_density)
    seen_shared = hand_over(among(after(seen_shared, change_shared), n_vel), half)

    seen = after(seen, change_shared).reshape(single, -1, width)
    seen_shared = in_order(seen_shared).reshape(elements - single, -1, width)
    table, incoming = cut_traces([(start_single, seen), (start_shared, seen_shared)])
    totals = hand_over(among(after(total, table), n_vel), n_vel)
    shared = after(shared, table)
    flux_shared = in_order(all_after(flux_shared, table))
    first, rest = stage_of(shared, flux_shared, change_shared, shared_jacobian)
    total_shared = collision(
        first,
        density=shared_density,
        base=((vel_id & half) * (width // span)).astype(jnp.int32).reshape(1),
        chunks=half,
        rest=rest,
        scale=0.5 * TIME_STEP,
    )
    totals_shared = hand_over(among(total_shared, half), half)
    (result,) = enter(table, all_after(incoming, total_shared), lift, 0.5 * TIME_STEP)
    for blocks, base, owned in ((totals_shared, single, shared_owned), (totals, 0, single_owned)):
        for step, block in enumerate(blocks):
            at = base + ((vel_id ^ step) & (len(blocks) - 1)) * owned
            block = block.reshape(owned, nodes, width)
            block = block + lax.dynamic_slice_in_dim(result, at, owned)
            result = lax.dynamic_update_slice_in_dim(result, block, at, 0)
    return result


def solution(mesh):
    in_specs = (
        P("space", None, "vel"),
        P("space", None, None),
        P("space", None),
        P(),
        P(),
        P("space", None, None),
        P("space", None),
    )
    out_specs = P("space", None, "vel")

    def step(*arguments):
        return body(mesh.shape["space"], mesh.shape["vel"], *arguments)

    return jax.shard_map(
        step, mesh=mesh, in_specs=in_specs, out_specs=out_specs, check_vma=False
    )
```

```python
import functools

import jax
import jax.numpy as jnp
import numpy as np
from jax import lax
from jax.experimental import pallas as pl
from jax.experimental.pallas import tpu as pltpu
from jax.sharding import PartitionSpec as P


VG = 16
SIDE = 4
FACES = 6
FACE_NODES = 16
LANES = 128

TIME_STEP = 0.03
LIFT_SCALE = 6.0


MIB = 1024 * 1024


def lagrange_derivative():
    points = np.array([-1.0, -1.0 / np.sqrt(5.0), 1.0 / np.sqrt(5.0), 1.0])
    barycentric = np.ones(4)
    for column in range(4):
        for second in range(4):
            if second != column:
                barycentric[column] = barycentric[column] / (points[column] - points[second])
    matrix = np.zeros((4, 4))
    for row_node in range(4):
        for col_node in range(4):
            if row_node != col_node:
                matrix[row_node, col_node] = (
                    barycentric[col_node]
                    / barycentric[row_node]
                    / (points[row_node] - points[col_node])
                )
        matrix[row_node, row_node] = -np.sum(matrix[row_node])
    return matrix


def derivative_parts():
    single = lagrange_derivative()
    identity = np.eye(4)
    stacked = np.concatenate(
        [
            np.kron(np.kron(single, identity), identity),
            np.kron(np.kron(identity, single), identity),
            np.kron(np.kron(identity, identity), single),
        ],
        0,
    ).astype(np.float32)
    high = stacked.astype(jnp.bfloat16)
    low = (stacked - high.astype(np.float32)).astype(jnp.bfloat16)
    return np.concatenate([high, high, low], 1)


def lift_parts():
    nodes = SIDE**3
    place = np.zeros((nodes, 3, 2, FACE_NODES), np.float32)
    for node in range(nodes):
        index = (node // 16, node // 4 % 4, node % 4)
        for direction in range(3):
            others = [index[d] for d in range(3) if d != direction]
            if index[direction] == 0:
                place[node, direction, 0, others[0] * 4 + others[1]] = 1.0
            if index[direction] == SIDE - 1:
                place[node, direction, 1, others[0] * 4 + others[1]] = 1.0
    place = place.reshape(nodes, 6 * FACE_NODES).astype(jnp.bfloat16)
    return np.concatenate([place, place], 1)


def shell():
    nodes = np.ndindex(SIDE, SIDE, SIDE)
    return [index for index in nodes if 0 in index]


SHELL = len(shell())
SHELL_MAIN = SHELL // 32 * 32
SHELL_ROWS = -(-SHELL // 8) * 8


def turned(index, flip):
    return tuple(SIDE - 1 - i if f else i for i, f in zip(index, flip))


def pack_parts():
    rows = {index: row for row, index in enumerate(shell())}
    pack = np.zeros((SHELL_ROWS, 3, 2, 2, FACE_NODES), np.float32)
    for direction in range(3):
        for first, second, a, b in np.ndindex(2, 2, SIDE, SIDE):
            where = list(turned((a, b), (first, second)))
            where.insert(direction, 0)
            pack[rows[tuple(where)], direction, first, second, a * SIDE + b] = 1.0
    pack = pack.reshape(SHELL_ROWS, -1).astype(jnp.bfloat16)
    return np.concatenate([pack, pack], 1)


def spread_parts():
    spread = np.zeros((SIDE, SIDE, SIDE, 2, 2, 2, SHELL_ROWS), np.float32)
    for flip in np.ndindex(2, 2, 2):
        for row, index in enumerate(shell()):
            spread[turned(index, flip) + flip + (row,)] = 1.0
    spread = spread.reshape(SIDE**3, -1).astype(jnp.bfloat16)
    return np.concatenate([spread, spread], 1)


def grid_velocities(first_id, amount):
    velocity_id = first_id + jnp.arange(amount, dtype=jnp.int32)
    components = [velocity_id // (VG * VG), velocity_id // VG % VG, velocity_id % VG]
    return jnp.stack(
        [3.0 * ((2.0 * component.astype(jnp.float32) + 1.0) / VG - 1.0) for component in components]
    )


def halves(value):
    high = value.astype(jnp.bfloat16)
    return high, (value - high.astype(jnp.float32)).astype(jnp.bfloat16)


def speeds_of(jacobian_ref, element, velocity):
    result = []
    for direction in range(3):
        base = element * 9 + direction * 3
        result.append(
            jacobian_ref[base] * velocity[0:1]
            + jacobian_ref[base + 1] * velocity[1:2]
            + jacobian_ref[base + 2] * velocity[2:3]
        )
    return result


def lifted(fluxes, speeds, lift):
    pieces = []
    for flux, speed in zip(fluxes, speeds):
        inward = speed > 0.0
        pieces.append(jnp.where(inward, flux, 0.0))
        pieces.append(jnp.where(inward, 0.0, flux))
    high, low = halves(jnp.concatenate(pieces, 0))
    return jnp.dot(lift, jnp.concatenate([high, low], 0), preferred_element_type=jnp.float32)


def signs(speeds):
    return [(jnp.where(s > 0.0, 1.0, 0.0), jnp.where(s > 0.0, 0.0, 1.0)) for s in speeds]


def packed(fluxes, speeds, pack):
    masks = signs(speeds)
    pieces = []
    for direction, flux in enumerate(fluxes):
        first, second = [masks[d] for d in range(3) if d != direction]
        pieces += [flux * (a * b) for a in first for b in second]
    high, low = halves(jnp.concatenate(pieces, 0))
    return jnp.dot(pack, jnp.concatenate([high, low], 0), preferred_element_type=jnp.float32)


def spread_out(rows, speeds, spread):
    masks = signs(speeds)
    pieces = [rows * (a * b * c) for a in masks[0] for b in masks[1] for c in masks[2]]
    high, low = halves(jnp.concatenate(pieces, 0))
    return jnp.dot(spread, jnp.concatenate([high, low], 0), preferred_element_type=jnp.float32)


def shell_rows(flux_ref, tail_ref, owned, element):
    for row in range(SHELL - SHELL_MAIN):
        at = owned * SHELL_MAIN + row * owned + element
        tail_ref[row : row + 1, :] = flux_ref[0, pl.ds(at, 1), :]
    for row in range(SHELL - SHELL_MAIN, tail_ref.shape[0]):
        tail_ref[row : row + 1, :] = jnp.zeros((1, tail_ref.shape[1]), jnp.float32)
    start = pl.multiple_of(element * SHELL_MAIN, SHELL_MAIN)
    return lambda lanes: jnp.concatenate(
        [flux_ref[0, pl.ds(start, SHELL_MAIN), lanes], tail_ref[:, lanes]], 0
    )


def own_flow(value, speeds, derivative):
    high, low = halves(value)
    slopes = jnp.dot(
        derivative, jnp.concatenate([high, low, high], 0), preferred_element_type=jnp.float32
    )
    node = lax.broadcasted_iota(jnp.int32, value.shape, 0)
    count = value.shape[0]
    total = None
    for direction in range(3):
        speed = speeds[direction]
        place = (node >> (4 - 2 * direction)) & 3
        side = jnp.where(speed > 0.0, 0, SIDE - 1)
        edge = jnp.where(place == side, LIFT_SCALE * jnp.abs(speed), 0.0)
        term = speed * slopes[direction * count : (direction + 1) * count] + edge * value
        total = term if total is None else total + term
    return -total


def lane_chunks(width):
    step = 2 * LANES if width % (2 * LANES) == 0 else LANES
    return [pl.ds(start, step) for start in range(0, width, step)]


def whole(space=pltpu.VMEM):
    return pl.BlockSpec(memory_space=space)


def params(mebibytes):
    return pltpu.CompilerParams(vmem_limit_bytes=mebibytes * MIB)


def cost(flops, moved):
    return pl.CostEstimate(flops=int(flops), bytes_accessed=int(moved), transcendentals=0)


def faces_kernel(cap, others, send_ref, *refs):
    value_ref = refs[0]
    change_ref = refs[1] if len(refs) > others + 2 else None
    table_ref, out_refs = refs[-1 - others], refs[len(refs) - others :]
    elements = value_ref.shape[0]
    surface = surface_nodes()

    def rows(element, start, stop):
        value = value_ref[element, start:stop, :]
        if change_ref is None:
            return value
        at = surface.index(start)
        return value + TIME_STEP * change_ref[element, at : at + stop - start, :]

    def build(element, carry):
        face = element * FACES
        table_ref[face] = rows(element, 0, 16)
        table_ref[face + 1] = rows(element, 48, 64)
        for i in range(SIDE):
            to = slice(4 * i, 4 * i + 4)
            table_ref[face + 2, to, :] = rows(element, 16 * i, 16 * i + 4)
            table_ref[face + 3, to, :] = rows(element, 16 * i + 12, 16 * i + 16)
        for m in range(FACE_NODES):
            to = slice(m, m + 1)
            table_ref[face + 4, to, :] = rows(element, 4 * m, 4 * m + 1)
            table_ref[face + 5, to, :] = rows(element, 4 * m + 3, 4 * m + 4)
        return carry

    lax.fori_loop(0, elements, build, 0)
    for number, out_ref in enumerate(out_refs):

        def pick(slot, carry, number=number, out_ref=out_ref):
            out_ref[slot] = table_ref[send_ref[number * cap + slot]]
            return carry

        lax.fori_loop(0, cap, pick, 0)


def faces(values, send_ids, others, cap):
    elements, _, width = values[0].shape
    out_shape = [jax.ShapeDtypeStruct((FACES * elements, FACE_NODES, width), jnp.float32)]
    out_shape += [jax.ShapeDtypeStruct((cap, FACE_NODES, width), jnp.float32)] * others
    moved = sum(value.size for value in values)
    moved += width * FACE_NODES * (FACES * elements + others * cap)
    return pl.pallas_call(
        functools.partial(faces_kernel, cap, others),
        out_shape=out_shape,
        in_specs=[whole(pltpu.SMEM)] + [whole()] * len(values),
        out_specs=[whole()] * (1 + others),
        compiler_params=params(44),
        cost_estimate=cost(0, 8 * moved),
        name="faces",
    )(send_ids, *values)


def inflow_kernel(scale, lookup_ref, jacobian_ref, velocity_ref, lift_ref, table_ref, in_ref, out_ref):
    local = table_ref.shape[0]
    remote = in_ref.shape[0]
    elements = local // FACES
    velocity = velocity_ref[...]

    def one(element, carry):
        speeds = speeds_of(jacobian_ref, element, velocity)
        fluxes = []
        for direction in range(3):
            traces = []
            for side in range(2):
                index = lookup_ref[element * FACES + 2 * direction + side]
                near = table_ref[jnp.minimum(index, local - 1)]
                far = in_ref[jnp.clip(index - local, 0, remote - 1)]
                far = jnp.where(index < local + remote, far, 0.0)
                traces.append(jnp.where(index < local, near, far))
            speed = speeds[direction]
            fluxes.append(
                (LIFT_SCALE * jnp.abs(speed)) * jnp.where(speed > 0.0, traces[0], traces[1])
            )
        if scale is None:
            owned = elements // out_ref.shape[0]
            owner, own = lax.div(element, owned), lax.rem(element, owned)
            rows = packed(fluxes, speeds, lift_ref[...])
            start = pl.multiple_of(own * SHELL_MAIN, SHELL_MAIN)
            out_ref[owner, pl.ds(start, SHELL_MAIN), :] = rows[:SHELL_MAIN]
            for row in range(SHELL_MAIN, SHELL):
                at = owned * SHELL_MAIN + (row - SHELL_MAIN) * owned + own
                out_ref[owner, pl.ds(at, 1), :] = rows[row : row + 1]
        else:
            out_ref[element] = scale * lifted(fluxes, speeds, lift_ref[...])
        return carry

    lax.fori_loop(0, elements, one, 0)


def inflow(table, incoming, lookup, jacobian, velocity, lift, scale, owners):
    width = table.shape[2]
    elements = table.shape[0] // FACES
    shape = (elements, SIDE**3, width)
    if scale is None:
        shape = (owners, elements // owners * SHELL, width)
    moved = table.size + incoming.size + np.prod(shape)
    return pl.pallas_call(
        functools.partial(inflow_kernel, scale),
        out_shape=jax.ShapeDtypeStruct(shape, jnp.float32),
        in_specs=[whole(pltpu.SMEM)] * 2 + [whole()] * 4,
        out_specs=whole(),
        compiler_params=params(36),
        cost_estimate=cost(0, 8 * moved),
        name="inflow",
    )(lookup, jacobian, velocity, lift, table, incoming)


def guess_kernel(
    owned, jacobian_ref, velocity_ref, derivative_ref, spread_ref, value_ref, flux_ref, out_ref, tail_ref
):
    element = pl.program_id(0)
    shell_of = shell_rows(flux_ref, tail_ref, owned, lax.rem(element, owned))
    for lanes in lane_chunks(value_ref.shape[2]):
        value = value_ref[0, :, lanes]
        speeds = speeds_of(jacobian_ref, element, velocity_ref[:, lanes])
        entering = spread_out(shell_of(lanes), speeds, spread_ref[...])
        flow = own_flow(value, speeds, derivative_ref[...]) + entering
        out_ref[0, :, lanes] = value + TIME_STEP * flow


def guess(value, flux, jacobian, velocity, derivative, spread):
    elements, nodes, width = value.shape
    owners, rows, _ = flux.shape
    owned = elements // owners
    return pl.pallas_call(
        functools.partial(guess_kernel, owned),
        grid=(elements,),
        out_shape=jax.ShapeDtypeStruct(value.shape, jnp.float32),
        in_specs=[
            whole(pltpu.SMEM),
            whole(),
            whole(),
            whole(),
            pl.BlockSpec((1, nodes, width), lambda e: (e, 0, 0)),
            pl.BlockSpec((1, rows, width), lambda e: (e // owned, 0, 0)),
        ],
        out_specs=pl.BlockSpec((1, nodes, width), lambda e: (e, 0, 0)),
        scratch_shapes=[pltpu.VMEM((SHELL_ROWS - SHELL_MAIN, width), jnp.float32)],
        compiler_params=params(16),
        cost_estimate=cost(2 * 256 * 192 * value.size // 64, 4 * (2 * value.size + flux.size)),
        name="guess",
    )(jacobian, velocity, derivative, spread, value, flux)


def stage_kernel(
    order_ref,
    jacobian_ref,
    velocity_ref,
    derivative_ref,
    spread_ref,
    value_ref,
    flux_ref,
    change_ref,
    first_ref,
    rest_ref,
    tail_ref,
):
    element = pl.program_id(1)
    shell_of = shell_rows(flux_ref, tail_ref, pl.num_programs(1), element)
    for lanes in lane_chunks(value_ref.shape[3]):
        value = value_ref[0, 0, :, lanes]
        speeds = speeds_of(jacobian_ref, element, velocity_ref[0, :, lanes])
        entering = spread_out(shell_of(lanes), speeds, spread_ref[...])
        flow = own_flow(value, speeds, derivative_ref[...]) + entering
        first = value + TIME_STEP * (flow + change_ref[0, 0, :, lanes])
        first_ref[0, 0, :, lanes] = first
        again = own_flow(first, speeds, derivative_ref[...])
        rest_ref[0, 0, :, lanes] = 0.5 * value + 0.5 * (first + TIME_STEP * again)


def stage(order, value, flux, change, jacobian, velocities, derivative, spread):
    chunks, elements, nodes, width = value.shape
    rows = flux.shape[1]
    block = pl.BlockSpec((1, 1, nodes, width), lambda c, e, order_ref: (order_ref[c], e, 0, 0))
    fixed = [
        pl.BlockSpec(part.shape, lambda c, e, order_ref: (0, 0)) for part in (derivative, spread)
    ]
    return pl.pallas_call(
        stage_kernel,
        grid_spec=pltpu.PrefetchScalarGridSpec(
            num_scalar_prefetch=1,
            grid=(chunks, elements),
            in_specs=[
                whole(pltpu.SMEM),
                pl.BlockSpec((1, 3, width), lambda c, e, order_ref: (order_ref[c], 0, 0)),
                *fixed,
                block,
                pl.BlockSpec((1, rows, width), lambda c, e, order_ref: (c, 0, 0)),
                block,
            ],
            out_specs=[block, block],
            scratch_shapes=[pltpu.VMEM((SHELL_ROWS - SHELL_MAIN, width), jnp.float32)],
        ),
        out_shape=[jax.ShapeDtypeStruct(value.shape, jnp.float32)] * 2,
        compiler_params=params(16),
        cost_estimate=cost(2 * 450 * 192 * value.size // 64, 4 * (4 * value.size + flux.size)),
        name="stage",
    )(order, jacobian, velocities, derivative, spread, value, flux, change)


def collide_kernel(slots, scale, column_ref, *refs):
    piece_refs = refs[:slots]
    weight_ref, density_ref = refs[slots : slots + 2]
    out_ref = refs[slots + 2 + (scale is not None)]
    pieces = [ref[0] for ref in piece_refs]
    high, low = halves(jnp.concatenate(pieces, 1))
    weight_high, weight_low = halves(
        jnp.concatenate([weight_ref[0, slot] for slot in range(slots)], 1)
    )

    def times(left, right):
        return lax.dot_general(
            left, right, (((1,), (1,)), ((), ())), preferred_element_type=jnp.float32
        )

    applied = times(high, weight_high) + (times(high, weight_low) + times(low, weight_high))
    change = density_ref[...] * (applied - pieces[0])
    if scale is None:
        out_ref[0] = change
        at = 0
        for start in range(0, out_ref.shape[1], SIDE**3):
            for a, b in surface_runs():
                refs[-1][0, at : at + b - a, :] = out_ref[0, start + a : start + b, :]
                at += b - a
    else:
        out_ref[0] = refs[slots + 2][0] + scale * change


def collide(value, weights, columns, density, rest=None, scale=None):
    _, rows, width = value.shape
    blocks, slots, span, _ = weights.shape
    per = width // span

    def piece(slot):
        def index(b, column_ref):
            column = column_ref[b * slots + slot]
            return (column // per, 0, column % per)

        return pl.BlockSpec((1, rows, span), index)

    def result(count):
        return pl.BlockSpec((1, count, span), lambda b, column_ref: (b // per, 0, b % per))

    out_specs, out_shape = result(rows), jax.ShapeDtypeStruct(value.shape, jnp.float32)
    if rest is None:
        seen = rows // SIDE**3 * len(surface_nodes())
        out_specs = [out_specs, result(seen)]
        out_shape = [out_shape, jax.ShapeDtypeStruct((value.shape[0], seen, width), jnp.float32)]
    in_specs = [piece(slot) for slot in range(slots)]
    in_specs.append(pl.BlockSpec((1, slots, span, span), lambda b, column_ref: (b, 0, 0, 0)))
    in_specs.append(pl.BlockSpec((rows, span), lambda b, column_ref: (0, 0)))
    operands = [value] * slots + [weights, density]
    if rest is not None:
        in_specs.append(out_specs)
        operands.append(rest)
    return pl.pallas_call(
        functools.partial(collide_kernel, slots, scale),
        grid_spec=pltpu.PrefetchScalarGridSpec(
            num_scalar_prefetch=1, grid=(blocks,), in_specs=in_specs, out_specs=out_specs
        ),
        out_shape=out_shape,
        compiler_params=params(24),
        cost_estimate=cost(
            12 * rows * blocks * slots * span * span,
            4 * (value.size * (slots + 1 + (rest is not None)) + weights.size),
        ),
        name="collide",
    )(columns, *operands)


def surface_runs():
    runs = []
    for node in range(SIDE**3):
        index = (node // 16, node // 4 % 4, node % 4)
        if any(i in (0, SIDE - 1) for i in index):
            if runs and runs[-1][1] == node:
                runs[-1][1] = node + 1
            else:
                runs.append([node, node + 1])
    return runs


def surface_nodes():
    return [node for a, b in surface_runs() for node in range(a, b)]


def after(value, other):
    return lax.optimization_barrier((value, other))[0]


def body(
    n_space,
    n_vel,
    distribution,
    inverse_jacobian,
    density,
    collision_blocks,
    block_columns,
    send_lists,
    exterior_faces,
):
    elements, nodes, width = distribution.shape
    owned = elements // n_vel
    rows = owned * nodes
    cap = send_lists.shape[2]
    local_faces = FACES * elements
    space_id = lax.axis_index("space")
    vel_id = lax.axis_index("vel")
    paired = n_space & (n_space - 1) == 0

    def partner(rank, step):
        return rank ^ step if paired else (rank + step) % n_space

    vel_paired = n_vel & (n_vel - 1) == 0

    def to_peer(rank, step):
        return rank ^ step if vel_paired else (rank + step) % n_vel

    def from_peer(rank, step):
        return rank ^ step if vel_paired else (rank - step) % n_vel

    def hand_over(value, wait_for_near=False):
        blocks = [
            lax.dynamic_index_in_dim(value, to_peer(vel_id, step), 0, False) for step in range(n_vel)
        ]
        blocks = list(lax.optimization_barrier(blocks))
        for step in range(1, n_vel):
            pairs = [(i, to_peer(i, step)) for i in range(n_vel)]
            blocks[step] = lax.ppermute(blocks[step], "vel", pairs)
            if step == 1 and wait_for_near:
                blocks[2:] = lax.optimization_barrier(blocks[1:])[1:]
        return blocks

    steps = range(1, n_space)
    send_rows = send_lists[0]
    send_ids = jnp.concatenate(
        [lax.dynamic_index_in_dim(send_rows, partner(space_id, step), 0, False) for step in steps]
    )
    lookup = exterior_faces.reshape(-1)
    source = (lookup - local_faces) // cap
    slot = (lookup - local_faces) % cap
    back = source ^ space_id if paired else (space_id - source) % n_space
    received = jnp.where(back == 0, 0, local_faces + (back - 1) * cap + slot)
    lookup = jnp.where(
        lookup < local_faces,
        lookup,
        jnp.where(
            lookup >= local_faces + n_space * cap, local_faces + (n_space - 1) * cap, received
        ),
    )

    jacobian = inverse_jacobian.reshape(-1)
    own_jacobian = lax.dynamic_slice_in_dim(jacobian, vel_id * owned * 9, owned * 9)
    own_density = lax.dynamic_slice_in_dim(density, vel_id * owned, owned).reshape(rows, 1)
    own_density = jnp.broadcast_to(own_density, (rows, collision_blocks.shape[2]))
    velocities = grid_velocities(0, n_vel * width).reshape(3, n_vel, width).transpose(1, 0, 2)
    velocity = grid_velocities(vel_id * width, width)
    columns = block_columns.reshape(-1)
    derivative = jnp.asarray(derivative_parts())
    lift = jnp.asarray(lift_parts())
    pack = jnp.asarray(pack_parts())
    spread = jnp.asarray(spread_parts())

    def exchange(value):
        return lax.all_to_all(value, "vel", split_axis=0, concat_axis=0, tiled=True)

    def neighbours(values, matrix, scale):
        table, *outgoing = faces(values, send_ids, n_space - 1, cap)
        incoming = jnp.concatenate(
            [
                lax.ppermute(out, "space", [(i, partner(i, step)) for i in range(n_space)])
                for step, out in zip(steps, outgoing)
            ]
        )
        return inflow(table, incoming, lookup, jacobian, velocity, matrix, scale, n_vel)

    value_own = exchange(distribution.reshape(n_vel, rows, width))
    flux = neighbours([distribution], pack, None)
    start = guess(distribution, flux, jacobian, velocity, derivative, spread)

    flux, start = lax.optimization_barrier((flux, start))
    flux_own = hand_over(flux, True)
    value_own = after(value_own, start)
    change, seen = collide(value_own, collision_blocks, columns, own_density)

    seen = exchange(seen)
    flux_own = jnp.stack(flux_own)
    shape = (n_vel, owned, nodes, width)
    first, rest = stage(
        jnp.stack([from_peer(vel_id, step) for step in range(n_vel)]),
        value_own.reshape(shape),
        flux_own,
        change.reshape(shape),
        own_jacobian,
        velocities,
        derivative,
        spread,
    )
    total = collide(
        first.reshape(n_vel, rows, width),
        collision_blocks,
        columns,
        own_density,
        rest.reshape(n_vel, rows, width),
        0.5 * TIME_STEP,
    )

    totals = hand_over(total)
    seen = after(seen, total)
    seen = seen.reshape(elements, -1, width)
    outer = neighbours([start, seen], lift, 0.5 * TIME_STEP)
    result = outer.reshape(n_vel, rows, width)
    for step, block in enumerate(totals):
        at = from_peer(vel_id, step)
        block = block + lax.dynamic_index_in_dim(result, at, 0, False)
        result = lax.dynamic_update_index_in_dim(result, block, at, 0)
    return result.reshape(distribution.shape)


def solution(mesh):
    in_specs = (
        P("space", None, "vel"),
        P("space", None, None),
        P("space", None),
        P(),
        P(),
        P("space", None, None),
        P("space", None),
    )
    out_specs = P("space", None, "vel")

    def step(*arguments):
        return body(mesh.shape["space"], mesh.shape["vel"], *arguments)

    return jax.shard_map(
        step, mesh=mesh, in_specs=in_specs, out_specs=out_specs, check_vma=False
    )
```
